512 devices in a mesh: tm: 128 (over y, x, z_lo, core), head: 4 (over z_hi).
Axes of the slice: x: 4, y: 8, z: 8 (z_hi: 4, z_lo: 2; z = z_hi * 2 + z_lo), core: 2. Of those that a mesh axis runs over, the one named last changes fastest.
Arguments:
- queries: bfloat16 [128, 128, 2048], P('tm', None, 'head'), may hold values from -6 to 6
- keys: bfloat16 [128, 128, 2048], P('tm', None, 'head'), may hold values from -6 to 6
- values: bfloat16 [128, 128, 2048], P('tm', None, 'head'), may hold values from -6 to 6
- anchor_of: int32 [128], replicated, may hold values from 0 to 126, as said below
- out_weight: bfloat16 [2048, 2048], P('head'), may hold values from -0.5 to 0.5
Outputs:
- mixed: bfloat16 [128, 128, 2048], P('tm', 'head')
The draws below stay inside these ranges and needn't reach their ends.
Inputs may be any that keep to these rules, and one draw needn't show every extreme that they name: anchor_of[f] is the first frame of the segment that holds frame f; segments are runs of 1 to 4 frames, one of exactly 4; frame 0 starts a segment and the last segment has exactly 2 frames.
All inputs are finite; a program needn't handle non-finite values.
Results may differ from the reference program's by a relative error of at most 0.013.
Values may be sent and summed in bfloat16 or wider, within the bound.
A program may use at most 128 MiB of HBM per device.

```python
import jax
import jax.numpy as jnp
from jax import lax

D = 2048
HEADS = 16
HS = 128
TOK = 128
SEGMAX = 4
FRAMES = 128
N_HEAD = 4


def draw_queries(key, part):
    shape = (FRAMES, TOK, HEADS * HS)
    base = jnp.clip(jax.random.normal(jax.random.fold_in(key, 1), shape, jnp.float32) * 1.4, -6.0, 6.0)
    return base.astype(jnp.bfloat16)


def draw_keys(key, part):
    shape = (FRAMES, TOK, HEADS * HS)
    base = jnp.clip(jax.random.normal(jax.random.fold_in(key, 2), shape, jnp.float32) * 1.4, -6.0, 6.0)
    return base.astype(jnp.bfloat16)


def draw_anchor_of(key, part):
    spans = jax.random.randint(jax.random.fold_in(key, 3), (FRAMES,), 1, SEGMAX + 1).astype(jnp.int32)
    lead_top = min(SEGMAX, FRAMES - SEGMAX - 2)
    lead = jax.random.randint(jax.random.fold_in(key, 4), (), 0, lead_top + 1).astype(jnp.int32)
    spans = spans.at[0].set(lead)
    spans = spans.at[1].set(SEGMAX)
    starts = jnp.cumsum(spans) - spans
    frame = jnp.arange(FRAMES, dtype=jnp.int32)
    flagged = jnp.any(starts[:, None] == frame[None, :], axis=0)
    flagged = flagged.at[0].set(True)
    flagged = flagged.at[FRAMES - 1].set(False)
    flagged = flagged.at[FRAMES - 2].set(True)
    return jax.lax.cummax(jnp.where(flagged, frame, 0), axis=0).astype(jnp.int32)


def shard_levels(rng, dims, split, low, high):
    level = 1.0
    for axis_at, parts in split:
        draws = jax.random.uniform(jax.random.fold_in(jax.random.fold_in(rng, 6), axis_at), (parts,), jnp.float32, low / len(split), high / len(split))
        level = level * jnp.repeat(jnp.exp(draws), dims[axis_at] // parts).reshape((-1,) + (1,) * (len(dims) - 1 - axis_at))
    return level


def bell_draw(key, dims, deviation, reach, split=(), held_as=jnp.bfloat16):
    entries = deviation * jax.random.normal(key, dims, jnp.float32)
    if split:
        entries = entries * shard_levels(key, dims, split, -0.22, 0.18)
    return jnp.clip(entries, -reach, reach).astype(held_as)


def setup_inputs(seed: int = 0) -> dict:
    arg_keys = jax.random.split(jax.random.key(seed), 6)
    return {
        "queries": draw_queries(jax.random.fold_in(arg_keys[5], 71), 0),
        "keys": draw_keys(jax.random.fold_in(arg_keys[5], 71), 0),
        "values": bell_draw(arg_keys[2], (FRAMES, TOK, HEADS * HS), 1.0, 6.0, ((0, 128), (2, 4))),
        "anchor_of": draw_anchor_of(jax.random.fold_in(arg_keys[5], 71), 0),
        "out_weight": bell_draw(arg_keys[4], (HEADS * HS, D), HS ** -0.5, 0.5, ((0, 4),)),
    }


def reference(queries, keys, values, anchor_of, out_weight):
    group = (HEADS // N_HEAD) * HS

    def one(frame):
        first = anchor_of[frame]
        before = jnp.maximum(frame - 1, 0)
        key_rows = jnp.concatenate([keys[frame], keys[before], keys[first]], 0)
        value_rows = jnp.concatenate([values[frame], values[before], values[first]], 0)
        query_rows = queries[frame].reshape(TOK, HEADS, HS).astype(jnp.float32)
        key_heads = key_rows.reshape(3 * TOK, HEADS, HS).astype(jnp.float32)
        value_heads = value_rows.reshape(3 * TOK, HEADS, HS).astype(jnp.float32)
        scores = jnp.einsum('qhd,khd->hqk', query_rows, key_heads) * (HS ** -0.5)
        block = jnp.arange(3 * TOK, dtype=jnp.int32) // TOK
        dist = frame - first
        present = (block == 0) | ((block == 1) & (dist >= 1)) | ((block == 2) & (dist >= 2))
        scores = jnp.where(present[None, None, :], scores, -jnp.inf)
        top = jnp.max(scores, axis=-1, keepdims=True)
        expo = jnp.exp(scores - top)
        weights = (expo / jnp.sum(expo, axis=-1, keepdims=True)).astype(jnp.bfloat16)
        attended = jnp.einsum('hqk,khd->qhd', weights.astype(jnp.float32), value_heads)
        attended = attended.astype(jnp.bfloat16).reshape(TOK, HEADS * HS)
        total = jnp.zeros((TOK, D), jnp.float32)
        for index in range(N_HEAD):
            part_sum = jnp.dot(attended[:, index * group:(index + 1) * group], out_weight[index * group:(index + 1) * group], preferred_element_type=jnp.float32)
            rounded = lax.optimization_barrier(part_sum.astype(jnp.bfloat16))
            total = total + rounded.astype(jnp.float32)
        return total.astype(jnp.bfloat16)

    return lax.map(one, jnp.arange(FRAMES, dtype=jnp.int32))
```

```python
import functools

import jax
import jax.numpy as jnp
from jax import lax
from jax.experimental import pallas as pl
from jax.experimental.pallas import tpu as pltpu
from jax.sharding import PartitionSpec as P

HS = 128
MESH = pl.DeviceIdType.MESH
F32 = jnp.float32
BF16 = jnp.bfloat16


def remote(src, dst, send_sem, recv_sem, device):
    return pltpu.make_async_remote_copy(
        src_ref=src,
        dst_ref=dst,
        send_sem=send_sem,
        recv_sem=recv_sem,
        device_id=device,
        device_id_type=MESH,
    )


def dot_nt(a, b):
    return lax.dot_general(a, b, (((1,), (1,)), ((), ())), preferred_element_type=F32)


def kernel(
    frames, groups,
    q_hbm, k_hbm, v_hbm, anchor_hbm, w_hbm, out_ref,
    anchor, q, own, prev, anc, pick, hand, w, att, acc, part, first, direct, chained, onward,
    load_sem, own_sem, w_sem,
    prev_send, prev_recv, pick_send, hand_send, anc_recv,
    first_send, first_recv, direct_send, direct_recv, chain_send, chain_recv,
):
    f = lax.axis_index("tm")
    h = lax.axis_index("head")
    tokens = q.shape[0]
    heads = q.shape[1] // HS
    chunks, _, width = part.shape
    rows = tokens // groups
    even = lax.rem(f, 2) == 0
    after, after2 = lax.rem(f + 1, frames), lax.rem(f + 2, frames)
    before, before2 = lax.rem(f + frames - 1, frames), lax.rem(f + frames - 2, frames)
    up, down = lax.rem(h + 1, groups), lax.rem(h + groups - 1, groups)
    far = lax.rem(h + 2, groups)

    barrier = pltpu.get_barrier_semaphore()
    for device in ((before, h), (f, up), (f, down)):
        pl.semaphore_signal(barrier, inc=1, device_id=device, device_id_type=MESH)

    @pl.when(even)
    def _():
        pl.semaphore_signal(barrier, inc=1, device_id=(before2, h), device_id_type=MESH)

    load_anchor = pltpu.make_async_copy(anchor_hbm, anchor, load_sem.at[0])
    load_q = pltpu.make_async_copy(q_hbm.at[0], q, load_sem.at[1])
    load_anchor.start()
    loads = []
    for c in range(heads):
        columns = pl.ds(c * HS, HS)
        loads.append([
            pltpu.make_async_copy(ref.at[0, :, columns], own.at[c, i], own_sem.at[c, i])
            for i, ref in enumerate((k_hbm, v_hbm))
        ])
        for copy in loads[-1]:
            copy.start()
    load_q.start()
    load_w = pltpu.make_async_copy(w_hbm, w, w_sem)
    load_w.start()

    pl.semaphore_wait(barrier, jnp.where(even, 4, 3))

    to_next = []
    for c in range(heads):
        columns = pl.ds(c * HS, HS)
        to_next.append([
            remote(ref.at[0, :, columns], prev.at[c, i], prev_send.at[c, i],
                   prev_recv.at[c, i], (after, h))
            for i, ref in enumerate((k_hbm, v_hbm))
        ])
        for copy in to_next[-1]:
            copy.start()

    load_anchor.wait()
    dist = f - anchor[f]
    next_dist = after - anchor[after]
    load_q.wait()
    scale = HS ** (-0.5)

    state = []
    picks = [remote(pick.at[c], anc.at[c], pick_send.at[c], anc_recv.at[c], (after2, h))
             for c in range(heads)]
    hands = [remote(hand.at[c], anc.at[c], hand_send.at[c], anc_recv.at[c], (after, h))
             for c in range(heads)]
    starts = jnp.full((tokens, HS), dist, jnp.int32) == 0
    for c in range(heads):
        for copy in loads[c]:
            copy.wait()
        for copy in to_next[c]:
            copy.wait_recv()

        @pl.when(even)
        def _():
            for i in range(2):
                pick[c, i] = jnp.where(starts, own[c, i], prev[c, i])
            picks[c].start()

    seen1 = jnp.full((tokens, tokens), dist, jnp.int32) >= 1
    seen2 = jnp.full((tokens, tokens), dist, jnp.int32) >= 2
    for c in range(heads):
        query = q[:, c * HS:(c + 1) * HS]
        s0 = dot_nt(query, own[c, 0]) * scale
        s1 = jnp.where(seen1, dot_nt(query, prev[c, 0]) * scale, -jnp.inf)
        top = jnp.max(jnp.maximum(s0, s1), axis=-1, keepdims=True)
        e0, e1 = jnp.exp(s0 - top), jnp.exp(s1 - top)
        total = jnp.sum(e0 + e1, axis=-1, keepdims=True)
        mixed = jnp.dot(e0.astype(BF16), own[c, 1], preferred_element_type=F32)
        mixed += jnp.dot(e1.astype(BF16), prev[c, 1], preferred_element_type=F32)
        state.append((top, total, mixed))

    takes_prev = jnp.full((tokens, HS), next_dist, jnp.int32) == 2
    for c in range(heads):
        picks[c].wait_recv()

        @pl.when(even)
        def _():
            for i in range(2):
                hand[c, i] = jnp.where(takes_prev, prev[c, i], anc[c, i])
            hands[c].start()

        query = q[:, c * HS:(c + 1) * HS]
        top, total, mixed = state[c]
        s2 = jnp.where(seen2, dot_nt(query, anc[c, 0]) * scale, -jnp.inf)
        peak = jnp.maximum(top, jnp.max(s2, axis=-1, keepdims=True))
        shrink = jnp.exp(top - peak)
        e2 = jnp.exp(s2 - peak)
        total = total * shrink + jnp.sum(e2, axis=-1, keepdims=True)
        mixed = mixed * shrink + jnp.dot(e2.astype(BF16), anc[c, 1], preferred_element_type=F32)
        att[:, c * HS:(c + 1) * HS] = (mixed / total).astype(BF16)
        if c == heads // 2:
            load_w.wait()
            half = (heads // 2) * HS
            for j in range(chunks):
                acc[j] = jnp.dot(att[:, :half], w[:half, j * width:(j + 1) * width],
                                 preferred_element_type=F32)

    def piece(group):
        return pl.ds(pl.multiple_of(group * rows, rows), rows)

    half = (heads // 2) * HS
    order = [j for pair in zip(range(chunks // 2), range(chunks // 2, chunks)) for j in pair]
    chain_to = [down if j < chunks // 2 else up for j in range(chunks)]
    direct_to = [up if j < chunks // 2 else down for j in range(chunks)]
    firsts = [remote(part.at[j, piece(far)], first.at[j], first_send.at[j], first_recv.at[j],
                     (f, chain_to[j])) for j in range(chunks)]
    directs = [remote(part.at[j, piece(direct_to[j])], direct.at[j], direct_send.at[j],
                      direct_recv.at[j], (f, direct_to[j])) for j in range(chunks)]
    chains = [remote(onward.at[j], chained.at[j], chain_send.at[j], chain_recv.at[j],
                     (f, chain_to[j])) for j in range(chunks)]
    for j in order:
        part[j] = (acc[j] + jnp.dot(att[:, half:], w[half:, j * width:(j + 1) * width],
                                    preferred_element_type=F32)).astype(BF16)
        firsts[j].start()
    for j in order:
        directs[j].start()
    for j in order:
        firsts[j].wait_recv()
        onward[j] = (part[j, piece(chain_to[j])].astype(F32) + first[j].astype(F32)).astype(BF16)
        chains[j].start()
    for j in order:
        directs[j].wait_recv()
        chains[j].wait_recv()
        out_ref[0, :, j * width:(j + 1) * width] = (
            part[j, piece(h)].astype(F32) + direct[j].astype(F32) + chained[j].astype(F32)
        ).astype(BF16)

    for c in range(heads):
        for copy in to_next[c]:
            copy.wait_send()
    for j in range(chunks):
        firsts[j].wait_send()
        directs[j].wait_send()
        chains[j].wait_send()

    @pl.when(even)
    def _():
        for c in range(heads):
            picks[c].wait_send()
            hands[c].wait_send()


def per_device(frames, groups, queries, keys, values, anchor_of, out_weight):
    _, tokens, wide = queries.shape
    heads = wide // HS
    depth, columns = out_weight.shape
    chunks = 4
    width = columns // chunks
    rows = tokens // groups
    block = pltpu.VMEM((heads, 2, tokens, HS), BF16)
    piece = pltpu.VMEM((chunks, rows, width), BF16)
    dma = pltpu.SemaphoreType.DMA
    hbm = pl.BlockSpec(memory_space=pl.ANY)
    return pl.pallas_call(
        functools.partial(kernel, frames, groups),
        out_shape=jax.ShapeDtypeStruct((1, rows, columns), BF16),
        in_specs=[hbm] * 5,
        out_specs=pl.BlockSpec(memory_space=pltpu.VMEM),
        scratch_shapes=[
            pltpu.SMEM(anchor_of.shape, jnp.int32),
            pltpu.VMEM((tokens, wide), BF16),
            block, block, block, block, block,
            pltpu.VMEM((depth, columns), BF16),
            pltpu.VMEM((tokens, wide), BF16),
            pltpu.VMEM((chunks, tokens, width), F32),
            pltpu.VMEM((chunks, tokens, width), BF16),
            piece, piece, piece, piece,
            dma((2,)), dma((heads, 2)), dma,
            dma((heads, 2)), dma((heads, 2)), dma((heads,)), dma((heads,)), dma((heads,)),
            dma((chunks,)), dma((chunks,)), dma((chunks,)), dma((chunks,)), dma((chunks,)),
            dma((chunks,)),
        ],
        compiler_params=pltpu.CompilerParams(collective_id=0, has_side_effects=True),
    )(queries, keys, values, anchor_of, out_weight)


def solution(mesh):
    placed = (
        P("tm", None, "head"),
        P("tm", None, "head"),
        P("tm", None, "head"),
        P(),
        P("head", None),
    )
    return jax.shard_map(
        functools.partial(per_device, mesh.shape["tm"], mesh.shape["head"]),
        mesh=mesh, in_specs=placed, out_specs=P("tm", "head", None), check_vma=False
    )
```

```python
import functools

import jax
import jax.numpy as jnp
from jax import lax
from jax.experimental import pallas as pl
from jax.experimental.pallas import tpu as pltpu
from jax.sharding import PartitionSpec as P

HS = 128
MESH = pl.DeviceIdType.MESH
F32 = jnp.float32
BF16 = jnp.bfloat16


def remote(src, dst, send_sem, recv_sem, device):
    return pltpu.make_async_remote_copy(
        src_ref=src,
        dst_ref=dst,
        send_sem=send_sem,
        recv_sem=recv_sem,
        device_id=device,
        device_id_type=MESH,
    )


def dot_nt(a, b):
    return lax.dot_general(a, b, (((1,), (1,)), ((), ())), preferred_element_type=F32)


def plan_of(me, low, high):
    a, b = low
    c, d = high
    P = [("P", j, None) for j in range(4)]
    if me == 0:
        return [P[a], ("D", a, 1), P[b], ("D", b, 1), P[c], ("D", c, 1), ("D", c, 3),
                P[d], ("D", d, 1), ("D", d, 3), ("F", a, None), ("F", c, None),
                ("F", b, None), ("F", d, None), ("C", a, 3), ("C", b, 3)]
    if me == 1:
        return [P[c], ("D", c, 0), P[d], ("D", d, 0), P[a], ("F", a, None), ("D", a, 2),
                P[b], ("D", b, 2), ("F", c, None), ("C", a, 0), ("C", b, 0),
                ("F", b, None), ("F", d, None), ("C", c, 2), ("C", d, 2)]
    if me == 2:
        return [P[a], ("F", a, None), P[c], ("F", c, None), P[b], ("F", b, None),
                P[d], ("F", d, None), ("D", a, 3), ("D", b, 3),
                ("C", a, 1), ("C", b, 1), ("C", c, 1), ("C", d, 1), ("C", c, 3), ("C", d, 3)]
    return [P[a], ("D", a, 0), ("F", a, None), P[b], ("D", b, 0), ("F", b, None),
            P[c], ("F", c, None), P[d], ("F", d, None), ("D", c, 2), ("D", d, 2),
            ("C", c, 0), ("C", d, 0), ("C", a, 2), ("C", b, 2)]


def kernel(
    frames, groups,
    q_hbm, k_hbm, v_hbm, anchor_hbm, w_hbm, mine_ref, direct_ref, chained_ref,
    anchor, q, own, prev, anc, pick, hand, w, att, acc, part, first, onward,
    load_sem, own_sem, w_sem, mine_sem,
    prev_send, prev_recv, pick_send, hand_send, anc_recv,
    first_send, first_recv, direct_send, direct_recv, chain_send, chain_recv,
):
    f = lax.axis_index("tm")
    h = lax.axis_index("head")
    tokens = q.shape[0]
    heads = q.shape[1] // HS
    chunks, _, width = part.shape
    rows = tokens // groups
    even = lax.rem(f, 2) == 0
    has_next, has_second = f < frames - 1, even & (f < frames - 2)
    after, after2 = lax.rem(f + 1, frames), lax.rem(f + 2, frames)
    up, down = lax.rem(h + 1, groups), lax.rem(h + groups - 1, groups)

    barrier = pltpu.get_barrier_semaphore()

    @pl.when(f > 0)
    def _():
        pl.semaphore_signal(barrier, inc=1, device_id=(f - 1, h), device_id_type=MESH)

    @pl.when(even & (f > 1))
    def _():
        pl.semaphore_signal(barrier, inc=1, device_id=(f - 2, h), device_id_type=MESH)

    for device in ((f, up), (f, down)):
        pl.semaphore_signal(barrier, inc=1, device_id=device, device_id_type=MESH)

    load_anchor = pltpu.make_async_copy(anchor_hbm, anchor, load_sem.at[0])
    load_q = pltpu.make_async_copy(q_hbm.at[0], q, load_sem.at[1])
    load_w = pltpu.make_async_copy(w_hbm, w, w_sem)
    loads = [[
        pltpu.make_async_copy(ref.at[0, :, pl.ds(c * HS, HS)], own.at[c, i], own_sem.at[c, i])
        for i, ref in enumerate((k_hbm, v_hbm))
    ] for c in range(heads)]
    for c in range(heads):
        for copy in loads[c]:
            copy.start()
    load_anchor.start()
    load_q.start()
    load_w.start()

    @pl.when(f == 0)
    def _():
        prev[...] = jnp.zeros_like(prev)

    @pl.when(f < 2)
    def _():
        anc[...] = jnp.zeros_like(anc)

    for c in range(heads):
        for copy in loads[c]:
            copy.wait()
    pl.semaphore_wait(
        barrier, 2 + jnp.where(has_next, 1, 0) + jnp.where(has_second, 1, 0))

    to_next = [remote(own.at[c], prev.at[c], prev_send.at[c], prev_recv.at[c], (after, h))
               for c in range(heads)]
    picks = [remote(pick.at[c], anc.at[c], pick_send.at[c], anc_recv.at[c], (after2, h))
             for c in range(heads)]
    hands = [remote(hand.at[c], anc.at[c], hand_send.at[c], anc_recv.at[c], (after, h))
             for c in range(heads)]

    @pl.when(has_next)
    def _():
        for c in range(heads):
            to_next[c].start()

    load_anchor.wait()
    dist = f - anchor[f]
    next_dist = after - anchor[after]
    load_q.wait()
    scale = HS ** (-0.5)

    starts = jnp.full((tokens, HS), dist, jnp.int32) == 0
    for c in range(heads):
        @pl.when(f > 0)
        def _():
            to_next[c].wait_recv()

        @pl.when(has_second)
        def _():
            for i in range(2):
                pick[c, i] = jnp.where(starts, own[c, i], prev[c, i])
            picks[c].start()

    seen1 = jnp.full((tokens, tokens), dist, jnp.int32) >= 1
    seen2 = jnp.full((tokens, tokens), dist, jnp.int32) >= 2
    state = []
    for c in range(heads):
        query = q[:, c * HS:(c + 1) * HS]
        s0 = dot_nt(query, own[c, 0]) * scale
        s1 = jnp.where(seen1, dot_nt(query, prev[c, 0]) * scale, -jnp.inf)
        top = jnp.max(jnp.maximum(s0, s1), axis=-1, keepdims=True)
        e0, e1 = jnp.exp(s0 - top), jnp.exp(s1 - top)
        total = jnp.sum(e0 + e1, axis=-1, keepdims=True)
        mixed = jnp.dot(e0.astype(BF16), own[c, 1], preferred_element_type=F32)
        mixed += jnp.dot(e1.astype(BF16), prev[c, 1], preferred_element_type=F32)
        state.append((top, total, mixed))

    takes_prev = jnp.full((tokens, HS), next_dist, jnp.int32) == 2
    half = (heads // 2) * HS

    def arrive_even(c):
        @pl.when(even & (f > 1))
        def _():
            picks[c].wait_recv()
            for i in range(2):
                hand[c, i] = jnp.where(takes_prev, prev[c, i], anc[c, i])
            hands[c].start()

    def arrive_odd(c):
        @pl.when(jnp.logical_not(even) & (f > 1))
        def _():
            hands[c].wait_recv()

    for c in range(heads):
        arrive_even(c)
        if c == heads - 1:
            load_w.wait()
            for j in range(chunks):
                acc[j] = jnp.dot(att[:, :half], w[:half, j * width:(j + 1) * width],
                                 preferred_element_type=F32)
        arrive_odd(c)
        query = q[:, c * HS:(c + 1) * HS]
        top, total, mixed = state[c]
        s2 = jnp.where(seen2, dot_nt(query, anc[c, 0]) * scale, -jnp.inf)
        peak = jnp.maximum(top, jnp.max(s2, axis=-1, keepdims=True))
        shrink = jnp.exp(top - peak)
        e2 = jnp.exp(s2 - peak)
        total = total * shrink + jnp.sum(e2, axis=-1, keepdims=True)
        mixed = mixed * shrink + jnp.dot(e2.astype(BF16), anc[c, 1], preferred_element_type=F32)
        att[:, c * HS:(c + 1) * HS] = (mixed / total).astype(BF16)

    def columns(j):
        return pl.ds(j * width, width)

    def reduce(me):
        upper, lower, far = (me + 1) % groups, (me - 1) % groups, (me + 2) % groups

        def via(dest, j):
            return (dest + 1) % groups if j < chunks // 2 or dest == 1 else (dest - 1) % groups

        def piece(j, dest):
            return part.at[j, pl.ds(dest * rows, rows)]

        def slot(at, dest):
            return 0 if dest == (at - 1) % groups else 1

        def first_copy(j, source):
            dest = (source + 2) % groups
            at = via(dest, j)
            n = slot(at, dest)
            return remote(piece(j, dest), first.at[n, j], first_send.at[j], first_recv.at[n, j],
                          (f, at))

        def direct_copy(j, dest):
            return remote(piece(j, dest), direct_ref.at[0, :, columns(j)],
                          direct_send.at[0 if dest == lower else 1, j], direct_recv.at[j],
                          (f, dest))

        def chain_copy(j, dest):
            n = slot(me, dest)
            return remote(onward.at[n, j], chained_ref.at[0, :, columns(j)], chain_send.at[n, j],
                          chain_recv.at[j], (f, dest))

        def project(j):
            part[j] = (acc[j] + jnp.dot(att[:, half:], w[half:, j * width:(j + 1) * width],
                                        preferred_element_type=F32)).astype(BF16)

        def chain(j, dest):
            n = slot(me, dest)
            first_copy(j, (dest + 2) % groups).wait_recv()
            onward[n, j] = (part[j, dest * rows:(dest + 1) * rows].astype(F32)
                            + first[n, j].astype(F32)).astype(BF16)
            copy = chain_copy(j, dest)
            copy.start()
            sent.append(copy)

        def go(copy):
            copy.start()
            sent.append(copy)

        sent = []
        everyone = range(chunks)
        low, high = everyone[:chunks // 2], everyone[chunks // 2:]
        directs = [(j, d) for d in (lower, upper) for j in everyone if via(d, j) != me]
        chains = [(j, d) for d in (lower, upper) for j in everyone if via(d, j) == me]
        plan = plan_of(me, low, high)
        done = set()
        for step in plan:
            kind, j, d = step
            if kind == "P":
                project(j)
            elif kind == "F":
                go(first_copy(j, me))
            elif kind == "D":
                assert (j, d) in directs
                go(direct_copy(j, d))
            else:
                assert (j, d) in chains
                chain(j, d)
            assert step not in done
            done.add(step)
        assert len(done) == 2 * chunks + len(directs) + len(chains)

        keep = pltpu.make_async_copy
        copies = [keep(piece(j, me), mine_ref.at[0, :, columns(j)], mine_sem.at[j])
                  for j in everyone]
        for copy in copies:
            copy.start()
        for copy in copies:
            copy.wait()
        for j in everyone:
            direct_copy(j, lower).wait_recv()
            chain_copy(j, lower).wait_recv()
        for copy in sent:
            copy.wait_send()

    for me in range(groups):
        pl.when(h == me)(functools.partial(reduce, me))

    @pl.when(has_next)
    def _():
        for c in range(heads):
            to_next[c].wait_send()

    @pl.when(has_second)
    def _():
        for c in range(heads):
            picks[c].wait_send()

    @pl.when(even & (f > 1))
    def _():
        for c in range(heads):
            hands[c].wait_send()


def per_device(frames, groups, queries, keys, values, anchor_of, out_weight):
    _, tokens, wide = queries.shape
    heads = wide // HS
    depth, columns = out_weight.shape
    chunks = 4
    width = columns // chunks
    rows = tokens // groups
    block = pltpu.VMEM((heads, 2, tokens, HS), BF16)
    pieces = pltpu.VMEM((2, chunks, rows, width), BF16)
    dma = pltpu.SemaphoreType.DMA
    hbm = pl.BlockSpec(memory_space=pltpu.HBM)
    anywhere = pl.BlockSpec(memory_space=pl.ANY)
    share = jax.ShapeDtypeStruct((1, rows, columns), BF16)
    mine, direct, chained = pl.pallas_call(
        functools.partial(kernel, frames, groups),
        out_shape=[share] * 3,
        in_specs=[hbm] * 5,
        out_specs=[anywhere] * 3,
        scratch_shapes=[
            pltpu.SMEM(anchor_of.shape, jnp.int32),
            pltpu.VMEM((tokens, wide), BF16),
            block, block, block, block, block,
            pltpu.VMEM((depth, columns), BF16),
            pltpu.VMEM((tokens, wide), BF16),
            pltpu.VMEM((chunks, tokens, width), F32),
            pltpu.VMEM((chunks, tokens, width), BF16),
            pieces, pieces,
            dma((2,)), dma((heads, 2)), dma, dma((chunks,)),
            dma((heads,)), dma((heads,)), dma((heads,)), dma((heads,)), dma((heads,)),
            dma((chunks,)), dma((2, chunks)), dma((2, chunks)), dma((chunks,)),
            dma((2, chunks)), dma((chunks,)),
        ],
        compiler_params=pltpu.CompilerParams(
            collective_id=0, has_side_effects=True, vmem_limit_bytes=24 * 2**20),
    )(*(pltpu.with_memory_space_constraint(x, pltpu.HBM)
        for x in (queries, keys, values, anchor_of, out_weight)))
    return (mine.astype(F32) + direct.astype(F32) + chained.astype(F32)).astype(BF16)


def solution(mesh):
    placed = (
        P("tm", None, "head"),
        P("tm", None, "head"),
        P("tm", None, "head"),
        P(),
        P("head", None),
    )
    return jax.shard_map(
        functools.partial(per_device, mesh.shape["tm"], mesh.shape["head"]),
        mesh=mesh, in_specs=placed, out_specs=P("tm", "head", None), check_vma=False
    )
```

```python
import functools

import jax
import jax.numpy as jnp
from jax import lax
from jax.experimental import pallas as pl
from jax.experimental.pallas import tpu as pltpu
from jax.sharding import PartitionSpec as P

HS = 128
MESH = pl.DeviceIdType.MESH
F32 = jnp.float32
BF16 = jnp.bfloat16


def remote(src, dst, send_sem, recv_sem, device):
    return pltpu.make_async_remote_copy(
        src_ref=src,
        dst_ref=dst,
        send_sem=send_sem,
        recv_sem=recv_sem,
        device_id=device,
        device_id_type=MESH,
    )


def dot_nt(a, b):
    return lax.dot_general(a, b, (((1,), (1,)), ((), ())), preferred_element_type=F32)


def plan_of(me, low, high):
    def project(js):
        return [("P", j, None) for j in js]

    def far(js):
        return [("F", j, None) for j in js]

    def near(js, dest):
        return [("D", j, dest) for j in js]

    def chain(js, dest):
        return [("C", j, dest) for j in js]

    def mix(*lists):
        return [step for group in zip(*lists) for step in group]

    cut = len(low) // 2
    if me == 0:
        return (mix(project(low), near(low, 1)) + mix(project(high), near(high, 1), near(high, 3))
                + mix(far(low), far(high)) + chain(low, 3))
    if me == 1:
        return (mix(project(high), near(high, 0)) + mix(project(low), near(low, 2))
                + far(low[:cut]) + far(high) + chain(low, 0) + far(low[cut:]) + chain(high, 2))
    if me == 2:
        return (mix(project(low), far(low), project(high), far(high)) + near(low, 3)
                + chain(low, 1) + chain(high, 1) + chain(high, 3))
    return (mix(project(low), near(low, 0), far(low)) + mix(project(high), far(high))
            + near(high, 2) + chain(high, 0) + chain(low, 2))


def kernel(
    frames, groups,
    q_hbm, k_hbm, v_hbm, anchor_hbm, w_hbm, mine_ref, direct_ref, chained_ref,
    anchor, q, own, prev, prev2, start, pick, w, att, acc, part, first, onward,
    load_sem, own_sem, w_sem, mine_sem,
    prev_send, prev_recv, prev2_send, prev2_recv, pick_send, start_send, start_recv, go_sem,
    first_send, first_recv, direct_send, direct_recv, chain_send, chain_recv,
):
    f = lax.axis_index("tm")
    h = lax.axis_index("head")
    tokens = q.shape[0]
    heads = q.shape[1] // HS
    chunks, _, width = part.shape
    rows = tokens // groups
    even = lax.rem(f, 2) == 0
    odd = jnp.logical_not(even)
    has_next, picking = f < frames - 1, even & (f < frames - 3)
    after, after3 = lax.rem(f + 1, frames), lax.rem(f + 3, frames)
    up, down = lax.rem(h + 1, groups), lax.rem(h + groups - 1, groups)

    barrier = pltpu.get_barrier_semaphore()

    @pl.when(f > 0)
    def _():
        pl.semaphore_signal(barrier, inc=1, device_id=(f - 1, h), device_id_type=MESH)

    @pl.when(odd & (f > 1))
    def _():
        pl.semaphore_signal(barrier, inc=1, device_id=(f - 3, h), device_id_type=MESH)

    @pl.when(even & (f > 1))
    def _():
        pl.semaphore_signal(barrier, inc=1, device_id=(f + 1, h), device_id_type=MESH)

    for device in ((f, up), (f, down)):
        pl.semaphore_signal(barrier, inc=1, device_id=device, device_id_type=MESH)

    load_anchor = pltpu.make_async_copy(anchor_hbm, anchor, load_sem.at[0])
    load_q = pltpu.make_async_copy(q_hbm.at[0], q, load_sem.at[1])
    load_w = pltpu.make_async_copy(w_hbm, w, w_sem)
    loads = [[
        pltpu.make_async_copy(ref.at[0, :, pl.ds(c * HS, HS)], own.at[c, i], own_sem.at[c, i])
        for i, ref in enumerate((k_hbm, v_hbm))
    ] for c in range(heads)]
    for c in range(heads):
        for copy in loads[c]:
            copy.start()
    load_anchor.start()
    load_q.start()
    load_w.start()

    @pl.when(f == 0)
    def _():
        prev[...] = jnp.zeros_like(prev)

    @pl.when(f < 2)
    def _():
        start[...] = jnp.zeros_like(start)

    for c in range(heads):
        for copy in loads[c]:
            copy.wait()
    pl.semaphore_wait(
        barrier, 2 + jnp.where(has_next, 1, 0) + jnp.where(picking, 1, 0)
        + jnp.where(odd & (f > 1), 1, 0))

    parts = [(c, i) for c in range(heads) for i in range(2)]
    to_next = {p: remote(own.at[p], prev.at[p], prev_send.at[p], prev_recv.at[p], (after, h))
               for p in parts}
    passing = {p: remote(prev.at[p], prev2.at[p], prev2_send.at[p], prev2_recv.at[p], (after, h))
               for p in parts}
    picks = {p: remote(pick.at[p], start.at[p], pick_send.at[p], start_recv.at[p], (after3, h))
             for p in parts}
    backs = {p: remote(start.at[p], start.at[p], start_send.at[p], start_recv.at[p],
                       (jnp.maximum(f - 1, 0), h)) for p in parts}

    @pl.when(has_next)
    def _():
        for p in parts:
            to_next[p].start()

    load_anchor.wait()
    dist = f - anchor[f]
    load_q.wait()
    scale = HS ** (-0.5)

    starts = jnp.full((tokens, HS), dist, jnp.int32) == 0
    for p in parts:
        @pl.when(f > 0)
        def _():
            to_next[p].wait_recv()

        @pl.when(picking)
        def _():
            pick[p] = jnp.where(starts, own[p], prev[p])
            picks[p].start()

        @pl.when(even & (f > 1))
        def _():
            passing[p].start()

    seen1 = jnp.full((tokens, tokens), dist, jnp.int32) >= 1
    seen2 = jnp.full((tokens, tokens), dist, jnp.int32) >= 2
    state = []
    for c in range(heads):
        query = q[:, c * HS:(c + 1) * HS]
        s0 = dot_nt(query, own[c, 0]) * scale
        s1 = jnp.where(seen1, dot_nt(query, prev[c, 0]) * scale, -jnp.inf)
        top = jnp.max(jnp.maximum(s0, s1), axis=-1, keepdims=True)
        e0, e1 = jnp.exp(s0 - top), jnp.exp(s1 - top)
        total = jnp.sum(e0 + e1, axis=-1, keepdims=True)
        mixed = jnp.dot(e0.astype(BF16), own[c, 1], preferred_element_type=F32)
        mixed += jnp.dot(e1.astype(BF16), prev[c, 1], preferred_element_type=F32)
        state.append((top, total, mixed))

    takes_prev = jnp.full((tokens, HS), jnp.where(odd, dist, 0), jnp.int32) == 2
    half = (heads // 2) * HS

    for c in range(heads):
        if c == heads - 1:
            load_w.wait()
            for j in range(chunks):
                acc[j] = jnp.dot(att[:, :half], w[:half, j * width:(j + 1) * width],
                                 preferred_element_type=F32)

        @pl.when(odd & (f > 1))
        def _():
            for i in range(2):
                picks[c, i].wait_recv()
                backs[c, i].start()
            for i in range(2):
                passing[c, i].wait_recv()

        @pl.when(even & (f > 1))
        def _():
            for i in range(2):
                backs[c, i].wait_recv()

        query = q[:, c * HS:(c + 1) * HS]
        top, total, mixed = state[c]
        anchor_key = jnp.where(takes_prev, prev2[c, 0], start[c, 0])
        anchor_value = jnp.where(takes_prev, prev2[c, 1], start[c, 1])
        s2 = jnp.where(seen2, dot_nt(query, anchor_key) * scale, -jnp.inf)
        peak = jnp.maximum(top, jnp.max(s2, axis=-1, keepdims=True))
        shrink = jnp.exp(top - peak)
        e2 = jnp.exp(s2 - peak)
        total = total * shrink + jnp.sum(e2, axis=-1, keepdims=True)
        mixed = mixed * shrink + jnp.dot(e2.astype(BF16), anchor_value, preferred_element_type=F32)
        att[:, c * HS:(c + 1) * HS] = (mixed / total).astype(BF16)

    @pl.when(has_next)
    def _():
        for p in parts:
            to_next[p].wait_send()

    @pl.when(picking)
    def _():
        for p in parts:
            picks[p].wait_send()

    @pl.when((f == 2) | (f == 3))
    def _():
        pl.semaphore_signal(go_sem, inc=1, device_id=(f - 2, h), device_id_type=MESH)

    @pl.when(f < 2)
    def _():
        pl.semaphore_wait(go_sem, 1)

    def columns(j):
        return pl.ds(j * width, width)

    def reduce(me):
        upper, lower, far = (me + 1) % groups, (me - 1) % groups, (me + 2) % groups

        def via(dest, j):
            return (dest + 1) % groups if j < chunks // 2 or dest == 1 else (dest - 1) % groups

        def piece(j, dest):
            return part.at[j, pl.ds(dest * rows, rows)]

        def slot(at, dest):
            return 0 if dest == (at - 1) % groups else 1

        def first_copy(j, source):
            dest = (source + 2) % groups
            at = via(dest, j)
            n = slot(at, dest)
            return remote(piece(j, dest), first.at[n, j], first_send.at[j], first_recv.at[n, j],
                          (f, at))

        def direct_copy(j, dest):
            return remote(piece(j, dest), direct_ref.at[0, :, columns(j)],
                          direct_send.at[0 if dest == lower else 1, j], direct_recv.at[j],
                          (f, dest))

        def chain_copy(j, dest):
            n = slot(me, dest)
            return remote(onward.at[n, j], chained_ref.at[0, :, columns(j)], chain_send.at[n, j],
                          chain_recv.at[j], (f, dest))

        def project(j):
            part[j] = (acc[j] + jnp.dot(att[:, half:], w[half:, j * width:(j + 1) * width],
                                        preferred_element_type=F32)).astype(BF16)

        def chain(j, dest):
            n = slot(me, dest)
            first_copy(j, (dest + 2) % groups).wait_recv()
            onward[n, j] = (part[j, dest * rows:(dest + 1) * rows].astype(F32)
                            + first[n, j].astype(F32)).astype(BF16)
            copy = chain_copy(j, dest)
            copy.start()
            sent.append(copy)

        def go(copy):
            copy.start()
            sent.append(copy)

        sent = []
        everyone = range(chunks)
        low, high = everyone[:chunks // 2], everyone[chunks // 2:]
        directs = [(j, d) for d in (lower, upper) for j in everyone if via(d, j) != me]
        chains = [(j, d) for d in (lower, upper) for j in everyone if via(d, j) == me]
        plan = plan_of(me, low, high)
        done = set()
        for step in plan:
            kind, j, d = step
            if kind == "P":
                project(j)
            elif kind == "F":
                go(first_copy(j, me))
            elif kind == "D":
                assert (j, d) in directs
                go(direct_copy(j, d))
            else:
                assert (j, d) in chains
                chain(j, d)
            assert step not in done
            done.add(step)
        assert len(done) == 2 * chunks + len(directs) + len(chains)

        keep = pltpu.make_async_copy
        copies = [keep(piece(j, me), mine_ref.at[0, :, columns(j)], mine_sem.at[j])
                  for j in everyone]
        for copy in copies:
            copy.start()
        for copy in copies:
            copy.wait()
        for j in everyone:
            direct_copy(j, lower).wait_recv()
            chain_copy(j, lower).wait_recv()
        for copy in sent:
            copy.wait_send()

    for me in range(groups):
        pl.when(h == me)(functools.partial(reduce, me))

    @pl.when(even & (f > 1))
    def _():
        for p in parts:
            passing[p].wait_send()

    @pl.when(odd & (f > 1))
    def _():
        for p in parts:
            backs[p].wait_send()


def per_device(frames, groups, queries, keys, values, anchor_of, out_weight):
    _, tokens, wide = queries.shape
    heads = wide // HS
    depth, columns = out_weight.shape
    chunks = 8
    width = columns // chunks
    rows = tokens // groups
    block = pltpu.VMEM((heads, 2, tokens, HS), BF16)
    pieces = pltpu.VMEM((2, chunks, rows, width), BF16)
    dma = pltpu.SemaphoreType.DMA
    hbm = pl.BlockSpec(memory_space=pltpu.HBM)
    anywhere = pl.BlockSpec(memory_space=pl.ANY)
    share = jax.ShapeDtypeStruct((1, rows, columns), BF16)
    mine, direct, chained = pl.pallas_call(
        functools.partial(kernel, frames, groups),
        out_shape=[share] * 3,
        in_specs=[hbm] * 5,
        out_specs=[anywhere] * 3,
        scratch_shapes=[
            pltpu.SMEM(anchor_of.shape, jnp.int32),
            pltpu.VMEM((tokens, wide), BF16),
            block, block, block, block, block,
            pltpu.VMEM((depth, columns), BF16),
            pltpu.VMEM((tokens, wide), BF16),
            pltpu.VMEM((chunks, tokens, width), F32),
            pltpu.VMEM((chunks, tokens, width), BF16),
            pieces, pieces,
            dma((2,)), dma((heads, 2)), dma, dma((chunks,)),
            *[dma((heads, 2))] * 7, pltpu.SemaphoreType.REGULAR,
            dma((chunks,)), dma((2, chunks)), dma((2, chunks)), dma((chunks,)),
            dma((2, chunks)), dma((chunks,)),
        ],
        compiler_params=pltpu.CompilerParams(
            collective_id=0, has_side_effects=True, vmem_limit_bytes=24 * 2**20),
    )(*(pltpu.with_memory_space_constraint(x, pltpu.HBM)
        for x in (queries, keys, values, anchor_of, out_weight)))
    return (mine.astype(F32) + direct.astype(F32) + chained.astype(F32)).astype(BF16)


def solution(mesh):
    placed = (
        P("tm", None, "head"),
        P("tm", None, "head"),
        P("tm", None, "head"),
        P(),
        P("head", None),
    )
    return jax.shard_map(
        functools.partial(per_device, mesh.shape["tm"], mesh.shape["head"]),
        mesh=mesh, in_specs=placed, out_specs=P("tm", "head", None), check_vma=False
    )
```

```python
import functools

import jax
import jax.numpy as jnp
from jax import lax
from jax.experimental import pallas as pl
from jax.experimental.pallas import tpu as pltpu
from jax.sharding import PartitionSpec as P

HS = 128
MESH = pl.DeviceIdType.MESH
F32 = jnp.float32
BF16 = jnp.bfloat16


def remote(src, dst, send_sem, recv_sem, device):
    return pltpu.make_async_remote_copy(
        src_ref=src,
        dst_ref=dst,
        send_sem=send_sem,
        recv_sem=recv_sem,
        device_id=device,
        device_id_type=MESH,
    )


def dot_nt(a, b):
    return lax.dot_general(a, b, (((1,), (1,)), ((), ())), preferred_element_type=F32)


def plan_of(me, low, high):
    def project(js):
        return [("P", j, None) for j in js]

    def far(js):
        return [("F", j, None) for j in js]

    def near(js, dest):
        return [("D", j, dest) for j in js]

    def chain(js, dest):
        return [("C", j, dest) for j in js]

    def mix(*lists):
        return [step for group in zip(*lists) for step in group]

    if me == 0:
        return (mix(project(high), far(high)) + mix(project(low), far(low))
                + near(low, 1) + near(high, 1) + near(high, 3) + chain(low, 3))
    if me == 1:
        return (mix(project(low), far(low)) + mix(project(high), near(high, 0), far(high))
                + near(low, 2) + chain(low, 0) + chain(high, 2))
    if me == 2:
        return (mix(project(low), far(low), project(high), far(high)) + near(low, 3)
                + chain(low, 1) + chain(high, 1) + chain(high, 3))
    return (mix(project(low), near(low, 0), far(low)) + mix(project(high), far(high))
            + near(high, 2) + chain(high, 0) + chain(low, 2))


def kernel(
    frames, groups,
    q_hbm, k_hbm, v_hbm, anchor_hbm, w_hbm, mine_ref, direct_ref, chained_ref,
    anchor, q, own, prev, prev2, start, pick, w, att, acc, part, first, onward,
    load_sem, own_sem, w_sem, mine_sem,
    prev_send, prev_recv, prev2_send, prev2_recv, pick_send, start_send, start_recv, go_sem,
    first_send, first_recv, direct_send, direct_recv, chain_send, chain_recv,
):
    f = lax.axis_index("tm")
    h = lax.axis_index("head")
    tokens = q.shape[0]
    heads = q.shape[1] // HS
    chunks, _, width = part.shape
    rows = tokens // groups
    even = lax.rem(f, 2) == 0
    odd = jnp.logical_not(even)
    has_next, picking = f < frames - 1, even & (f < frames - 3)
    after, after3 = lax.rem(f + 1, frames), lax.rem(f + 3, frames)
    up, down = lax.rem(h + 1, groups), lax.rem(h + groups - 1, groups)

    barrier = pltpu.get_barrier_semaphore()

    @pl.when(f > 0)
    def _():
        pl.semaphore_signal(barrier, inc=1, device_id=(f - 1, h), device_id_type=MESH)

    @pl.when(odd & (f > 1))
    def _():
        pl.semaphore_signal(barrier, inc=1, device_id=(f - 3, h), device_id_type=MESH)

    @pl.when(even & (f > 1))
    def _():
        pl.semaphore_signal(barrier, inc=1, device_id=(f + 1, h), device_id_type=MESH)

    for device in ((f, up), (f, down)):
        pl.semaphore_signal(barrier, inc=1, device_id=device, device_id_type=MESH)

    load_anchor = pltpu.make_async_copy(anchor_hbm, anchor, load_sem.at[0])
    load_q = pltpu.make_async_copy(q_hbm.at[0], q, load_sem.at[1])
    load_w = pltpu.make_async_copy(w_hbm, w, w_sem)
    loads = [[
        pltpu.make_async_copy(ref.at[0, :, pl.ds(c * HS, HS)], own.at[c, i], own_sem.at[c, i])
        for i, ref in enumerate((k_hbm, v_hbm))
    ] for c in range(heads)]
    for c in range(heads):
        for copy in loads[c]:
            copy.start()
    load_anchor.start()
    load_q.start()
    load_w.start()

    @pl.when(f == 0)
    def _():
        prev[...] = jnp.zeros_like(prev)

    @pl.when(f < 2)
    def _():
        start[...] = jnp.zeros_like(start)

    for c in range(heads):
        for copy in loads[c]:
            copy.wait()
    pl.semaphore_wait(
        barrier, 2 + jnp.where(has_next, 1, 0) + jnp.where(picking, 1, 0)
        + jnp.where(odd & (f > 1), 1, 0))

    parts = [(c, i) for c in range(heads) for i in range(2)]
    to_next = {p: remote(own.at[p], prev.at[p], prev_send.at[p], prev_recv.at[p], (after, h))
               for p in parts}
    passing = {p: remote(prev.at[p], prev2.at[p], prev2_send.at[p], prev2_recv.at[p], (after, h))
               for p in parts}
    picks = {p: remote(pick.at[p], start.at[p], pick_send.at[p], start_recv.at[p], (after3, h))
             for p in parts}
    backs = {p: remote(start.at[p], start.at[p], start_send.at[p], start_recv.at[p],
                       (jnp.maximum(f - 1, 0), h)) for p in parts}

    @pl.when(has_next)
    def _():
        for p in parts:
            to_next[p].start()

    load_anchor.wait()
    dist = f - anchor[f]
    load_q.wait()
    scale = HS ** (-0.5)

    starts = jnp.full((tokens, HS), dist, jnp.int32) == 0
    for p in parts:
        @pl.when(f > 0)
        def _():
            to_next[p].wait_recv()

        @pl.when(picking)
        def _():
            pick[p] = jnp.where(starts, own[p], prev[p])
            picks[p].start()

        @pl.when(even & (f > 1))
        def _():
            passing[p].start()

    seen1 = jnp.full((tokens, tokens), dist, jnp.int32) >= 1
    seen2 = jnp.full((tokens, tokens), dist, jnp.int32) >= 2
    state = []
    for c in range(heads):
        query = q[:, c * HS:(c + 1) * HS]
        s0 = dot_nt(query, own[c, 0]) * scale
        s1 = jnp.where(seen1, dot_nt(query, prev[c, 0]) * scale, -jnp.inf)
        top = jnp.max(jnp.maximum(s0, s1), axis=-1, keepdims=True)
        e0, e1 = jnp.exp(s0 - top), jnp.exp(s1 - top)
        total = jnp.sum(e0 + e1, axis=-1, keepdims=True)
        mixed = jnp.dot(e0.astype(BF16), own[c, 1], preferred_element_type=F32)
        mixed += jnp.dot(e1.astype(BF16), prev[c, 1], preferred_element_type=F32)
        state.append((top, total, mixed))

    takes_prev = jnp.full((tokens, HS), jnp.where(odd, dist, 0), jnp.int32) == 2
    half = (heads // 2) * HS

    for c in range(heads):
        if c == heads - 1:
            load_w.wait()
            for j in range(chunks):
                acc[j] = jnp.dot(att[:, :half], w[:half, j * width:(j + 1) * width],
                                 preferred_element_type=F32)

        @pl.when(odd & (f > 1))
        def _():
            for i in range(2):
                picks[c, i].wait_recv()
                backs[c, i].start()
            for i in range(2):
                passing[c, i].wait_recv()

        @pl.when(even & (f > 1))
        def _():
            for i in range(2):
                backs[c, i].wait_recv()

        query = q[:, c * HS:(c + 1) * HS]
        top, total, mixed = state[c]
        anchor_key = jnp.where(takes_prev, prev2[c, 0], start[c, 0])
        anchor_value = jnp.where(takes_prev, prev2[c, 1], start[c, 1])
        s2 = jnp.where(seen2, dot_nt(query, anchor_key) * scale, -jnp.inf)
        peak = jnp.maximum(top, jnp.max(s2, axis=-1, keepdims=True))
        shrink = jnp.exp(top - peak)
        e2 = jnp.exp(s2 - peak)
        total = total * shrink + jnp.sum(e2, axis=-1, keepdims=True)
        mixed = mixed * shrink + jnp.dot(e2.astype(BF16), anchor_value, preferred_element_type=F32)
        att[:, c * HS:(c + 1) * HS] = (mixed / total).astype(BF16)

    @pl.when(has_next)
    def _():
        for p in parts:
            to_next[p].wait_send()

    @pl.when(picking)
    def _():
        for p in parts:
            picks[p].wait_send()

    @pl.when((f == 2) | (f == 3))
    def _():
        pl.semaphore_signal(go_sem, inc=1, device_id=(f - 2, h), device_id_type=MESH)

    @pl.when(f < 2)
    def _():
        pl.semaphore_wait(go_sem, 1)

    def columns(j):
        return pl.ds(j * width, width)

    def reduce(me):
        upper, lower, far = (me + 1) % groups, (me - 1) % groups, (me + 2) % groups

        def via(dest, j):
            return (dest + 1) % groups if j < chunks // 2 or dest == 1 else (dest - 1) % groups

        def piece(j, dest):
            return part.at[j, pl.ds(dest * rows, rows)]

        def slot(at, dest):
            return 0 if dest == (at - 1) % groups else 1

        def first_copy(j, source):
            dest = (source + 2) % groups
            at = via(dest, j)
            n = slot(at, dest)
            return remote(piece(j, dest), first.at[n, j], first_send.at[j], first_recv.at[n, j],
                          (f, at))

        def direct_copy(j, dest):
            return remote(piece(j, dest), direct_ref.at[0, :, columns(j)],
                          direct_send.at[0 if dest == lower else 1, j], direct_recv.at[j],
                          (f, dest))

        def chain_copy(j, dest):
            n = slot(me, dest)
            return remote(onward.at[n, j], chained_ref.at[0, :, columns(j)], chain_send.at[n, j],
                          chain_recv.at[j], (f, dest))

        def project(j):
            part[j] = (acc[j] + jnp.dot(att[:, half:], w[half:, j * width:(j + 1) * width],
                                        preferred_element_type=F32)).astype(BF16)

        def chain(j, dest):
            n = slot(me, dest)
            first_copy(j, (dest + 2) % groups).wait_recv()
            onward[n, j] = (part[j, dest * rows:(dest + 1) * rows].astype(F32)
                            + first[n, j].astype(F32)).astype(BF16)
            copy = chain_copy(j, dest)
            copy.start()
            sent.append(copy)

        def go(copy):
            copy.start()
            sent.append(copy)

        sent = []
        everyone = range(chunks)
        low, high = everyone[:chunks // 2], everyone[chunks // 2:]
        directs = [(j, d) for d in (lower, upper) for j in everyone if via(d, j) != me]
        chains = [(j, d) for d in (lower, upper) for j in everyone if via(d, j) == me]
        plan = plan_of(me, low, high)
        done = set()
        for step in plan:
            kind, j, d = step
            if kind == "P":
                project(j)
            elif kind == "F":
                go(first_copy(j, me))
            elif kind == "D":
                assert (j, d) in directs
                go(direct_copy(j, d))
            else:
                assert (j, d) in chains
                chain(j, d)
            assert step not in done
            done.add(step)
        assert len(done) == 2 * chunks + len(directs) + len(chains)

        keep = pltpu.make_async_copy
        copies = [keep(piece(j, me), mine_ref.at[0, :, columns(j)], mine_sem.at[j])
                  for j in everyone]
        for copy in copies:
            copy.start()
        for copy in copies:
            copy.wait()
        for j in everyone:
            direct_copy(j, lower).wait_recv()
            chain_copy(j, lower).wait_recv()
        for copy in sent:
            copy.wait_send()

    for me in range(groups):
        pl.when(h == me)(functools.partial(reduce, me))

    @pl.when(even & (f > 1))
    def _():
        for p in parts:
            passing[p].wait_send()

    @pl.when(odd & (f > 1))
    def _():
        for p in parts:
            backs[p].wait_send()


def per_device(frames, groups, queries, keys, values, anchor_of, out_weight):
    _, tokens, wide = queries.shape
    heads = wide // HS
    depth, columns = out_weight.shape
    chunks = 8
    width = columns // chunks
    rows = tokens // groups
    block = pltpu.VMEM((heads, 2, tokens, HS), BF16)
    pieces = pltpu.VMEM((2, chunks, rows, width), BF16)
    dma = pltpu.SemaphoreType.DMA
    hbm = pl.BlockSpec(memory_space=pltpu.HBM)
    anywhere = pl.BlockSpec(memory_space=pl.ANY)
    share = jax.ShapeDtypeStruct((1, rows, columns), BF16)
    mine, direct, chained = pl.pallas_call(
        functools.partial(kernel, frames, groups),
        out_shape=[share] * 3,
        in_specs=[hbm] * 5,
        out_specs=[anywhere] * 3,
        scratch_shapes=[
            pltpu.SMEM(anchor_of.shape, jnp.int32),
            pltpu.VMEM((tokens, wide), BF16),
            block, block, block, block, block,
            pltpu.VMEM((depth, columns), BF16),
            pltpu.VMEM((tokens, wide), BF16),
            pltpu.VMEM((chunks, tokens, width), F32),
            pltpu.VMEM((chunks, tokens, width), BF16),
            pieces, pieces,
            dma((2,)), dma((heads, 2)), dma, dma((chunks,)),
            *[dma((heads, 2))] * 7, pltpu.SemaphoreType.REGULAR,
            dma((chunks,)), dma((2, chunks)), dma((2, chunks)), dma((chunks,)),
            dma((2, chunks)), dma((chunks,)),
        ],
        compiler_params=pltpu.CompilerParams(
            collective_id=0, has_side_effects=True, vmem_limit_bytes=24 * 2**20),
    )(*(pltpu.with_memory_space_constraint(x, pltpu.HBM)
        for x in (queries, keys, values, anchor_of, out_weight)))
    return (mine.astype(F32) + direct.astype(F32) + chained.astype(F32)).astype(BF16)


def solution(mesh):
    placed = (
        P("tm", None, "head"),
        P("tm", None, "head"),
        P("tm", None, "head"),
        P(),
        P("head", None),
    )
    return jax.shard_map(
        functools.partial(per_device, mesh.shape["tm"], mesh.shape["head"]),
        mesh=mesh, in_specs=placed, out_specs=P("tm", "head", None), check_vma=False
    )
```

```python
import functools

import jax
import jax.numpy as jnp
from jax import lax
from jax.experimental import pallas as pl
from jax.experimental.pallas import tpu as pltpu
from jax.sharding import PartitionSpec as P

HS = 128
MESH = pl.DeviceIdType.MESH
F32 = jnp.float32
BF16 = jnp.bfloat16


def remote(src, dst, send_sem, recv_sem, device):
    return pltpu.make_async_remote_copy(
        src_ref=src,
        dst_ref=dst,
        send_sem=send_sem,
        recv_sem=recv_sem,
        device_id=device,
        device_id_type=MESH,
    )


def dot_nt(a, b):
    return lax.dot_general(a, b, (((1,), (1,)), ((), ())), preferred_element_type=F32)


def plan_of(me, low, high):
    def project(js):
        return [("P", j, None) for j in js]

    def far(js):
        return [("F", j, None) for j in js]

    def near(js, dest):
        return [("D", j, dest) for j in js]

    def chain(js, dest):
        return [("C", j, dest) for j in js]

    def mix(*lists):
        return [step for group in zip(*lists) for step in group]

    if me == 0:
        return (mix(project(high), far(high)) + mix(project(low), far(low))
                + near(low, 1) + near(high[:-1], 1) + near(high, 3) + chain(high[-1:], 1)
                + chain(low, 3))
    if me == 1:
        return (mix(project(low), far(low)) + mix(project(high), near(high, 0), far(high))
                + near(low, 2) + chain(low, 0) + chain(high, 2))
    if me == 2:
        return (mix(project(low), far(low), project(high), far(high)) + near(low, 3)
                + near(high[-1:], 1) + chain(low, 1) + chain(high[:-1], 1) + chain(high, 3))
    return (mix(project(low), near(low, 0), far(low)) + mix(project(high), far(high))
            + near(high, 2) + chain(high, 0) + chain(low, 2))


def kernel(
    frames, groups,
    q_hbm, k_hbm, v_hbm, anchor_hbm, w_hbm, mine_ref, direct_ref, chained_ref,
    anchor, q, own, prev, prev2, start, pick, w, att, acc, part, first, onward,
    load_sem, own_sem, w_sem, mine_sem,
    prev_send, prev_recv, prev2_send, prev2_recv, pick_send, start_send, start_recv, go_sem,
    first_send, first_recv, direct_send, direct_recv, chain_send, chain_recv,
):
    f = lax.axis_index("tm")
    h = lax.axis_index("head")
    tokens = q.shape[0]
    heads = q.shape[1] // HS
    chunks, _, width = part.shape
    rows = tokens // groups
    even = lax.rem(f, 2) == 0
    odd = jnp.logical_not(even)
    has_next, picking = f < frames - 1, even & (f < frames - 3)
    after, after3 = lax.rem(f + 1, frames), lax.rem(f + 3, frames)
    up, down = lax.rem(h + 1, groups), lax.rem(h + groups - 1, groups)

    barrier = pltpu.get_barrier_semaphore()

    @pl.when(f > 0)
    def _():
        pl.semaphore_signal(barrier, inc=1, device_id=(f - 1, h), device_id_type=MESH)

    @pl.when(odd & (f > 1))
    def _():
        pl.semaphore_signal(barrier, inc=1, device_id=(f - 3, h), device_id_type=MESH)

    @pl.when(even & (f > 1))
    def _():
        pl.semaphore_signal(barrier, inc=1, device_id=(f + 1, h), device_id_type=MESH)

    for device in ((f, up), (f, down)):
        pl.semaphore_signal(barrier, inc=1, device_id=device, device_id_type=MESH)

    load_anchor = pltpu.make_async_copy(anchor_hbm, anchor, load_sem.at[0])
    load_q = pltpu.make_async_copy(q_hbm.at[0], q, load_sem.at[1])
    load_w = pltpu.make_async_copy(w_hbm, w, w_sem)
    loads = [[
        pltpu.make_async_copy(ref.at[0, :, pl.ds(c * HS, HS)], own.at[c, i], own_sem.at[c, i])
        for i, ref in enumerate((k_hbm, v_hbm))
    ] for c in range(heads)]
    for c in range(heads):
        for copy in loads[c]:
            copy.start()
    load_anchor.start()
    load_q.start()
    load_w.start()

    @pl.when(f == 0)
    def _():
        prev[...] = jnp.zeros_like(prev)

    @pl.when(f < 2)
    def _():
        start[...] = jnp.zeros_like(start)

    for c in range(heads):
        for copy in loads[c]:
            copy.wait()
    pl.semaphore_wait(
        barrier, 2 + jnp.where(has_next, 1, 0) + jnp.where(picking, 1, 0)
        + jnp.where(odd & (f > 1), 1, 0))

    parts = [(c, i) for c in range(heads) for i in range(2)]
    to_next = {p: remote(own.at[p], prev.at[p], prev_send.at[p], prev_recv.at[p], (after, h))
               for p in parts}
    passing = {p: remote(prev.at[p], prev2.at[p], prev2_send.at[p], prev2_recv.at[p], (after, h))
               for p in parts}
    picks = {p: remote(pick.at[p], start.at[p], pick_send.at[p], start_recv.at[p], (after3, h))
             for p in parts}
    backs = {p: remote(start.at[p], start.at[p], start_send.at[p], start_recv.at[p],
                       (jnp.maximum(f - 1, 0), h)) for p in parts}

    @pl.when(has_next)
    def _():
        for p in parts:
            to_next[p].start()

    load_anchor.wait()
    dist = f - anchor[f]
    load_q.wait()
    scale = HS ** (-0.5)

    starts = jnp.full((tokens, HS), dist, jnp.int32) == 0
    for p in parts:
        @pl.when(f > 0)
        def _():
            to_next[p].wait_recv()

        @pl.when(picking)
        def _():
            pick[p] = jnp.where(starts, own[p], prev[p])
            picks[p].start()

        @pl.when(even & (f > 1))
        def _():
            passing[p].start()

    seen1 = jnp.full((tokens, tokens), dist, jnp.int32) >= 1
    seen2 = jnp.full((tokens, tokens), dist, jnp.int32) >= 2
    state = []
    for c in range(heads):
        query = q[:, c * HS:(c + 1) * HS]
        s0 = dot_nt(query, own[c, 0]) * scale
        s1 = jnp.where(seen1, dot_nt(query, prev[c, 0]) * scale, -jnp.inf)
        top = jnp.max(jnp.maximum(s0, s1), axis=-1, keepdims=True)
        e0, e1 = jnp.exp(s0 - top), jnp.exp(s1 - top)
        total = jnp.sum(e0 + e1, axis=-1, keepdims=True)
        mixed = jnp.dot(e0.astype(BF16), own[c, 1], preferred_element_type=F32)
        mixed += jnp.dot(e1.astype(BF16), prev[c, 1], preferred_element_type=F32)
        state.append((top, total, mixed))

    takes_prev = jnp.full((tokens, HS), jnp.where(odd, dist, 0), jnp.int32) == 2
    half = (heads // 2) * HS

    for c in range(heads):
        if c == heads - 1:
            load_w.wait()
            for j in range(chunks):
                acc[j] = jnp.dot(att[:, :half], w[:half, j * width:(j + 1) * width],
                                 preferred_element_type=F32)

        @pl.when(odd & (f > 1))
        def _():
            for i in range(2):
                picks[c, i].wait_recv()
                backs[c, i].start()
            for i in range(2):
                passing[c, i].wait_recv()

        @pl.when(even & (f > 1))
        def _():
            for i in range(2):
                backs[c, i].wait_recv()

        query = q[:, c * HS:(c + 1) * HS]
        top, total, mixed = state[c]
        anchor_key = jnp.where(takes_prev, prev2[c, 0], start[c, 0])
        anchor_value = jnp.where(takes_prev, prev2[c, 1], start[c, 1])
        s2 = jnp.where(seen2, dot_nt(query, anchor_key) * scale, -jnp.inf)
        peak = jnp.maximum(top, jnp.max(s2, axis=-1, keepdims=True))
        shrink = jnp.exp(top - peak)
        e2 = jnp.exp(s2 - peak)
        total = total * shrink + jnp.sum(e2, axis=-1, keepdims=True)
        mixed = mixed * shrink + jnp.dot(e2.astype(BF16), anchor_value, preferred_element_type=F32)
        att[:, c * HS:(c + 1) * HS] = (mixed / total).astype(BF16)

    @pl.when(has_next)
    def _():
        for p in parts:
            to_next[p].wait_send()

    @pl.when(picking)
    def _():
        for p in parts:
            picks[p].wait_send()

    @pl.when((f == 2) | (f == 3))
    def _():
        pl.semaphore_signal(go_sem, inc=1, device_id=(f - 2, h), device_id_type=MESH)

    @pl.when(f < 2)
    def _():
        pl.semaphore_wait(go_sem, 1)

    def columns(j):
        return pl.ds(j * width, width)

    def reduce(me):
        upper, lower, far = (me + 1) % groups, (me - 1) % groups, (me + 2) % groups

        def via(dest, j):
            onward_up = j >= (chunks - 1 if dest == 1 else chunks // 2)
            return (dest - 1 if onward_up else dest + 1) % groups

        def piece(j, dest):
            return part.at[j, pl.ds(dest * rows, rows)]

        def slot(at, dest):
            return 0 if dest == (at - 1) % groups else 1

        def first_copy(j, source):
            dest = (source + 2) % groups
            at = via(dest, j)
            n = slot(at, dest)
            return remote(piece(j, dest), first.at[n, j], first_send.at[j], first_recv.at[n, j],
                          (f, at))

        def direct_copy(j, dest):
            return remote(piece(j, dest), direct_ref.at[0, :, columns(j)],
                          direct_send.at[0 if dest == lower else 1, j], direct_recv.at[j],
                          (f, dest))

        def chain_copy(j, dest):
            n = slot(me, dest)
            return remote(onward.at[n, j], chained_ref.at[0, :, columns(j)], chain_send.at[n, j],
                          chain_recv.at[j], (f, dest))

        def project(j):
            part[j] = (acc[j] + jnp.dot(att[:, half:], w[half:, j * width:(j + 1) * width],
                                        preferred_element_type=F32)).astype(BF16)

        def chain(j, dest):
            n = slot(me, dest)
            first_copy(j, (dest + 2) % groups).wait_recv()
            onward[n, j] = (part[j, dest * rows:(dest + 1) * rows].astype(F32)
                            + first[n, j].astype(F32)).astype(BF16)
            copy = chain_copy(j, dest)
            copy.start()
            sent.append(copy)

        def go(copy):
            copy.start()
            sent.append(copy)

        sent = []
        everyone = range(chunks)
        low, high = everyone[:chunks // 2], everyone[chunks // 2:]
        directs = [(j, d) for d in (lower, upper) for j in everyone if via(d, j) != me]
        chains = [(j, d) for d in (lower, upper) for j in everyone if via(d, j) == me]
        plan = plan_of(me, low, high)
        done = set()
        for step in plan:
            kind, j, d = step
            if kind == "P":
                project(j)
            elif kind == "F":
                go(first_copy(j, me))
            elif kind == "D":
                assert (j, d) in directs
                go(direct_copy(j, d))
            else:
                assert (j, d) in chains
                chain(j, d)
            assert step not in done
            done.add(step)
        assert len(done) == 2 * chunks + len(directs) + len(chains)

        keep = pltpu.make_async_copy
        copies = [keep(piece(j, me), mine_ref.at[0, :, columns(j)], mine_sem.at[j])
                  for j in everyone]
        for copy in copies:
            copy.start()
        for copy in copies:
            copy.wait()
        for j in everyone:
            direct_copy(j, lower).wait_recv()
            chain_copy(j, lower).wait_recv()
        for copy in sent:
            copy.wait_send()

    for me in range(groups):
        pl.when(h == me)(functools.partial(reduce, me))

    @pl.when(even & (f > 1))
    def _():
        for p in parts:
            passing[p].wait_send()

    @pl.when(odd & (f > 1))
    def _():
        for p in parts:
            backs[p].wait_send()


def per_device(frames, groups, queries, keys, values, anchor_of, out_weight):
    _, tokens, wide = queries.shape
    heads = wide // HS
    depth, columns = out_weight.shape
    chunks = 8
    width = columns // chunks
    rows = tokens // groups
    block = pltpu.VMEM((heads, 2, tokens, HS), BF16)
    pieces = pltpu.VMEM((2, chunks, rows, width), BF16)
    dma = pltpu.SemaphoreType.DMA
    hbm = pl.BlockSpec(memory_space=pltpu.HBM)
    anywhere = pl.BlockSpec(memory_space=pl.ANY)
    share = jax.ShapeDtypeStruct((1, rows, columns), BF16)
    mine, direct, chained = pl.pallas_call(
        functools.partial(kernel, frames, groups),
        out_shape=[share] * 3,
        in_specs=[hbm] * 5,
        out_specs=[anywhere] * 3,
        scratch_shapes=[
            pltpu.SMEM(anchor_of.shape, jnp.int32),
            pltpu.VMEM((tokens, wide), BF16),
            block, block, block, block, block,
            pltpu.VMEM((depth, columns), BF16),
            pltpu.VMEM((tokens, wide), BF16),
            pltpu.VMEM((chunks, tokens, width), F32),
            pltpu.VMEM((chunks, tokens, width), BF16),
            pieces, pieces,
            dma((2,)), dma((heads, 2)), dma, dma((chunks,)),
            *[dma((heads, 2))] * 7, pltpu.SemaphoreType.REGULAR,
            dma((chunks,)), dma((2, chunks)), dma((2, chunks)), dma((chunks,)),
            dma((2, chunks)), dma((chunks,)),
        ],
        compiler_params=pltpu.CompilerParams(
            collective_id=0, has_side_effects=True, vmem_limit_bytes=24 * 2**20),
    )(*(pltpu.with_memory_space_constraint(x, pltpu.HBM)
        for x in (queries, keys, values, anchor_of, out_weight)))
    return (mine.astype(F32) + direct.astype(F32) + chained.astype(F32)).astype(BF16)


def solution(mesh):
    placed = (
        P("tm", None, "head"),
        P("tm", None, "head"),
        P("tm", None, "head"),
        P(),
        P("head", None),
    )
    return jax.shard_map(
        functools.partial(per_device, mesh.shape["tm"], mesh.shape["head"]),
        mesh=mesh, in_specs=placed, out_specs=P("tm", "head", None), check_vma=False
    )
```

```python
import functools

import jax
import jax.numpy as jnp
from jax import lax
from jax.experimental import pallas as pl
from jax.experimental.pallas import tpu as pltpu
from jax.sharding import PartitionSpec as P

HS = 128
MESH = pl.DeviceIdType.MESH
F32 = jnp.float32
BF16 = jnp.bfloat16


def remote(src, dst, send_sem, recv_sem, device):
    return pltpu.make_async_remote_copy(
        src_ref=src,
        dst_ref=dst,
        send_sem=send_sem,
        recv_sem=recv_sem,
        device_id=device,
        device_id_type=MESH,
    )


def dot_nt(a, b):
    return lax.dot_general(a, b, (((1,), (1,)), ((), ())), preferred_element_type=F32)


def plan_of(me, low, high):
    def project(js):
        return [("P", j, None) for j in js]

    def far(js):
        return [("F", j, None) for j in js]

    def near(js, dest):
        return [("D", j, dest) for j in js]

    def chain(js, dest):
        return [("C", j, dest) for j in js]

    def mix(*lists):
        return [step for group in zip(*lists) for step in group]

    if me == 0:
        return (mix(project(high), far(high)) + mix(project(low), far(low))
                + near(low, 1) + near(high[:-1], 1) + near(high, 3) + chain(high[-1:], 1)
                + chain(low, 3))
    if me == 1:
        return (mix(project(low), far(low)) + mix(project(high), near(high, 0), far(high))
                + near(low, 2) + chain(low, 0) + chain(high, 2))
    if me == 2:
        return (mix(project(low), far(low), project(high), far(high)) + near(low, 3)
                + near(high[-1:], 1) + chain(low, 1) + chain(high[:-1], 1) + chain(high, 3))
    return (mix(project(low), near(low, 0), far(low)) + mix(project(high), far(high))
            + near(high, 2) + chain(high, 0) + chain(low, 2))


def kernel(
    frames, groups,
    q_hbm, k_hbm, v_hbm, anchor_hbm, w_hbm, mine_ref, direct_ref, chained_ref,
    anchor, q, own, prev, prev2, start, pick, w, att, acc, part, first, onward,
    load_sem, own_sem, w_sem, mine_sem,
    prev_send, prev_recv, prev2_send, prev2_recv, pick_send, start_send, start_recv, go_sem,
    first_send, first_recv, direct_send, direct_recv, chain_send, chain_recv,
):
    f = lax.axis_index("tm")
    h = lax.axis_index("head")
    tokens = q.shape[0]
    heads = q.shape[1] // HS
    chunks, _, width = acc.shape
    rows = tokens // groups
    even = lax.rem(f, 2) == 0
    odd = jnp.logical_not(even)
    has_next, picking = f < frames - 1, even & (f < frames - 3)
    after, after3 = lax.rem(f + 1, frames), lax.rem(f + 3, frames)
    up, down = lax.rem(h + 1, groups), lax.rem(h + groups - 1, groups)

    barrier = pltpu.get_barrier_semaphore()

    @pl.when(f > 0)
    def _():
        pl.semaphore_signal(barrier, inc=1, device_id=(f - 1, h), device_id_type=MESH)

    @pl.when(odd & (f > 1))
    def _():
        pl.semaphore_signal(barrier, inc=1, device_id=(f - 3, h), device_id_type=MESH)

    @pl.when(even & (f > 1))
    def _():
        pl.semaphore_signal(barrier, inc=1, device_id=(f + 1, h), device_id_type=MESH)

    for device in ((f, up), (f, down)):
        pl.semaphore_signal(barrier, inc=1, device_id=device, device_id_type=MESH)

    load_anchor = pltpu.make_async_copy(anchor_hbm, anchor, load_sem.at[0])
    load_q = pltpu.make_async_copy(q_hbm.at[0], q, load_sem.at[1])
    load_w = pltpu.make_async_copy(w_hbm, w, w_sem)
    loads = [[
        pltpu.make_async_copy(ref.at[0, :, pl.ds(c * HS, HS)], own.at[c, i], own_sem.at[c, i])
        for i, ref in enumerate((k_hbm, v_hbm))
    ] for c in range(heads)]
    for c in range(heads):
        for copy in loads[c]:
            copy.start()
    load_anchor.start()
    load_q.start()
    load_w.start()

    @pl.when(f == 0)
    def _():
        prev[...] = jnp.zeros_like(prev)

    @pl.when(f < 2)
    def _():
        start[...] = jnp.zeros_like(start)

    for c in range(heads):
        for copy in loads[c]:
            copy.wait()
    pl.semaphore_wait(
        barrier, 2 + jnp.where(has_next, 1, 0) + jnp.where(picking, 1, 0)
        + jnp.where(odd & (f > 1), 1, 0))

    parts = [(c, i) for c in range(heads) for i in range(2)]
    to_next = [remote(own.at[c], prev.at[c], prev_send.at[c], prev_recv.at[c], (after, h))
               for c in range(heads)]
    passing = [remote(prev.at[c], prev2.at[c], prev2_send.at[c], prev2_recv.at[c], (after, h))
               for c in range(heads)]
    picks = [remote(pick.at[c], start.at[c], pick_send.at[c], start_recv.at[c], (after3, h))
             for c in range(heads)]
    backs = [remote(start.at[c], start.at[c], start_send.at[c], start_recv.at[c],
                    (jnp.maximum(f - 1, 0), h)) for c in range(heads)]

    @pl.when(has_next)
    def _():
        for copy in to_next:
            copy.start()

    load_anchor.wait()
    dist = f - anchor[f]
    load_q.wait()
    scale = HS ** (-0.5)

    starts = jnp.full((tokens, HS), dist, jnp.int32) == 0
    for p in parts:
        if p[1] == 0:
            @pl.when(f > 0)
            def _():
                to_next[p[0]].wait_recv()

        @pl.when(picking)
        def _():
            pick[p] = jnp.where(starts, own[p], prev[p])
            if p[1] == 1:
                picks[p[0]].start()

        if p[1] == 1:
            @pl.when(even & (f > 1))
            def _():
                passing[p[0]].start()

    seen1 = jnp.full((tokens, tokens), dist, jnp.int32) >= 1
    seen2 = jnp.full((tokens, tokens), dist, jnp.int32) >= 2
    state = []
    for c in range(heads):
        query = q[:, c * HS:(c + 1) * HS]
        s0 = dot_nt(query, own[c, 0]) * scale
        s1 = jnp.where(seen1, dot_nt(query, prev[c, 0]) * scale, -jnp.inf)
        top = jnp.max(jnp.maximum(s0, s1), axis=-1, keepdims=True)
        e0, e1 = jnp.exp(s0 - top), jnp.exp(s1 - top)
        total = jnp.sum(e0 + e1, axis=-1, keepdims=True)
        mixed = jnp.dot(e0.astype(BF16), own[c, 1], preferred_element_type=F32)
        mixed += jnp.dot(e1.astype(BF16), prev[c, 1], preferred_element_type=F32)
        state.append((top, total, mixed))

    takes_prev = jnp.full((tokens, HS), jnp.where(odd, dist, 0), jnp.int32) == 2
    half = (heads // 2) * HS

    for c in range(heads):
        if c == heads - 1:
            load_w.wait()
            for j in range(chunks):
                acc[j] = jnp.dot(att[:, :half], w[:half, j * width:(j + 1) * width],
                                 preferred_element_type=F32)

        @pl.when(odd & (f > 1))
        def _():
            picks[c].wait_recv()
            backs[c].start()
            passing[c].wait_recv()

        @pl.when(even & (f > 1))
        def _():
            backs[c].wait_recv()

        query = q[:, c * HS:(c + 1) * HS]
        top, total, mixed = state[c]
        anchor_key = jnp.where(takes_prev, prev2[c, 0], start[c, 0])
        anchor_value = jnp.where(takes_prev, prev2[c, 1], start[c, 1])
        s2 = jnp.where(seen2, dot_nt(query, anchor_key) * scale, -jnp.inf)
        peak = jnp.maximum(top, jnp.max(s2, axis=-1, keepdims=True))
        shrink = jnp.exp(top - peak)
        e2 = jnp.exp(s2 - peak)
        total = total * shrink + jnp.sum(e2, axis=-1, keepdims=True)
        mixed = mixed * shrink + jnp.dot(e2.astype(BF16), anchor_value, preferred_element_type=F32)
        att[:, c * HS:(c + 1) * HS] = (mixed / total).astype(BF16)

    @pl.when(has_next)
    def _():
        for copy in to_next:
            copy.wait_send()

    @pl.when(picking)
    def _():
        for copy in picks:
            copy.wait_send()

    @pl.when((f == 2) | (f == 3))
    def _():
        pl.semaphore_signal(go_sem, inc=1, device_id=(f - 2, h), device_id_type=MESH)

    @pl.when(f < 2)
    def _():
        pl.semaphore_wait(go_sem, 1)

    def columns(j):
        return pl.ds(j * width, width)

    def reduce(me):
        upper, lower, far = (me + 1) % groups, (me - 1) % groups, (me + 2) % groups

        def via(dest, j):
            onward_up = j >= (chunks - 1 if dest == 1 else chunks // 2)
            return (dest - 1 if onward_up else dest + 1) % groups

        def piece(j, dest):
            return part.at[pl.ds(dest * rows, rows), columns(j)]

        def slot(at, dest):
            return 0 if dest == (at - 1) % groups else 1

        def first_copy(j, source):
            dest = (source + 2) % groups
            at = via(dest, j)
            n = slot(at, dest)
            return remote(piece(j, dest), first.at[n, :, columns(j)], first_send.at[j], first_recv.at[n, j],
                          (f, at))

        def direct_copy(run, dest):
            at = pl.ds(run[0] * width, len(run) * width)
            return remote(part.at[pl.ds(dest * rows, rows), at], direct_ref.at[0, :, at],
                          direct_send.at[0 if dest == lower else 1, run[0]],
                          direct_recv.at[run[0]], (f, dest))

        def runs_to(dest):
            source = [(dest - 1) % groups if via(dest, j) != (dest - 1) % groups
                      else (dest + 1) % groups for j in everyone]
            runs = []
            for j in everyone:
                if runs and len(runs[-1]) < 4 and source[runs[-1][0]] == source[j]:
                    runs[-1].append(j)
                else:
                    runs.append([j])
            return runs

        def chain_copy(j, dest):
            n = slot(me, dest)
            return remote(onward.at[n, :, columns(j)], chained_ref.at[0, :, columns(j)], chain_send.at[n, j],
                          chain_recv.at[j], (f, dest))

        def project(j):
            part[:, j * width:(j + 1) * width] = (acc[j] + jnp.dot(att[:, half:], w[half:, j * width:(j + 1) * width],
                                        preferred_element_type=F32)).astype(BF16)

        def chain(j, dest):
            n = slot(me, dest)
            first_copy(j, (dest + 2) % groups).wait_recv()
            at = slice(j * width, (j + 1) * width)
            onward[n, :, at] = (part[dest * rows:(dest + 1) * rows, at].astype(F32)
                                + first[n, :, at].astype(F32)).astype(BF16)
            copy = chain_copy(j, dest)
            copy.start()
            sent.append(copy)

        def go(copy):
            copy.start()
            sent.append(copy)

        sent, waiting = [], []
        everyone = range(chunks)
        low, high = everyone[:chunks // 2], everyone[chunks // 2:]
        directs = [(j, d) for d in (lower, upper) for j in everyone if via(d, j) != me]
        chains = [(j, d) for d in (lower, upper) for j in everyone if via(d, j) == me]
        plan = plan_of(me, low, high)
        done = set()
        for step in plan:
            kind, j, d = step
            if kind == "P":
                project(j)
            elif kind == "F":
                go(first_copy(j, me))
            elif kind == "D":
                assert (j, d) in directs
                waiting.append((j, d))
                run = next(r for r in runs_to(d) if j in r)
                if all((k, d) in waiting for k in run):
                    go(direct_copy(run, d))
            else:
                assert (j, d) in chains
                chain(j, d)
            assert step not in done
            done.add(step)
        assert len(done) == 2 * chunks + len(directs) + len(chains)

        keep = pltpu.make_async_copy
        copy = keep(part.at[pl.ds(me * rows, rows)], mine_ref.at[0], mine_sem)
        copy.start()
        copy.wait()
        for run in runs_to(me):
            at = pl.ds(run[0] * width, len(run) * width)
            remote(part.at[pl.ds(me * rows, rows), at], direct_ref.at[0, :, at],
                   direct_send.at[0, run[0]], direct_recv.at[run[0]], (f, lower)).wait_recv()
        for j in everyone:
            chain_copy(j, lower).wait_recv()
        for copy in sent:
            copy.wait_send()

    for me in range(groups):
        pl.when(h == me)(functools.partial(reduce, me))

    @pl.when(even & (f > 1))
    def _():
        for copy in passing:
            copy.wait_send()

    @pl.when(odd & (f > 1))
    def _():
        for copy in backs:
            copy.wait_send()


def per_device(frames, groups, queries, keys, values, anchor_of, out_weight):
    _, tokens, wide = queries.shape
    heads = wide // HS
    depth, columns = out_weight.shape
    chunks = 8
    width = columns // chunks
    rows = tokens // groups
    block = pltpu.VMEM((heads, 2, tokens, HS), BF16)
    pieces = pltpu.VMEM((2, rows, columns), BF16)
    dma = pltpu.SemaphoreType.DMA
    hbm = pl.BlockSpec(memory_space=pltpu.HBM)
    anywhere = pl.BlockSpec(memory_space=pl.ANY)
    share = jax.ShapeDtypeStruct((1, rows, columns), BF16)
    mine, direct, chained = pl.pallas_call(
        functools.partial(kernel, frames, groups),
        out_shape=[share] * 3,
        in_specs=[hbm] * 5,
        out_specs=[anywhere] * 3,
        scratch_shapes=[
            pltpu.SMEM(anchor_of.shape, jnp.int32),
            pltpu.VMEM((tokens, wide), BF16),
            block, block, block, block, block,
            pltpu.VMEM((depth, columns), BF16),
            pltpu.VMEM((tokens, wide), BF16),
            pltpu.VMEM((chunks, tokens, width), F32),
            pltpu.VMEM((tokens, columns), BF16),
            pieces, pieces,
            dma((2,)), dma((heads, 2)), dma, dma,
            *[dma((heads,))] * 7, pltpu.SemaphoreType.REGULAR,
            dma((chunks,)), dma((2, chunks)), dma((2, chunks)), dma((chunks,)),
            dma((2, chunks)), dma((chunks,)),
        ],
        compiler_params=pltpu.CompilerParams(
            collective_id=0, has_side_effects=True, vmem_limit_bytes=24 * 2**20),
    )(*(pltpu.with_memory_space_constraint(x, pltpu.HBM)
        for x in (queries, keys, values, anchor_of, out_weight)))
    return (mine.astype(F32) + direct.astype(F32) + chained.astype(F32)).astype(BF16)


def solution(mesh):
    placed = (
        P("tm", None, "head"),
        P("tm", None, "head"),
        P("tm", None, "head"),
        P(),
        P("head", None),
    )
    return jax.shard_map(
        functools.partial(per_device, mesh.shape["tm"], mesh.shape["head"]),
        mesh=mesh, in_specs=placed, out_specs=P("tm", "head", None), check_vma=False
    )
```

```python
import functools

import jax
import jax.numpy as jnp
from jax import lax
from jax.experimental import pallas as pl
from jax.experimental.pallas import tpu as pltpu
from jax.sharding import PartitionSpec as P

HS = 128
MESH = pl.DeviceIdType.MESH
F32 = jnp.float32
BF16 = jnp.bfloat16


def remote(src, dst, send_sem, recv_sem, device):
    return pltpu.make_async_remote_copy(
        src_ref=src,
        dst_ref=dst,
        send_sem=send_sem,
        recv_sem=recv_sem,
        device_id=device,
        device_id_type=MESH,
    )


def dot_nt(a, b):
    return lax.dot_general(a, b, (((1,), (1,)), ((), ())), preferred_element_type=F32)


def plan_of(me, low, high):
    def project(js):
        return [("P", j, None) for j in js]

    def far(js):
        return [("F", j, None) for j in js]

    def near(js, dest):
        return [("D", j, dest) for j in js]

    def chain(js, dest):
        return [("C", j, dest) for j in js]

    def mix(*lists):
        return [step for group in zip(*lists) for step in group]

    if me == 0:
        return (mix(project(high), far(high)) + mix(project(low), far(low))
                + near(low, 1) + near(high[:-1], 1) + near(high, 3) + chain(high[-1:], 1)
                + chain(low, 3))
    if me == 1:
        return (mix(project(low), far(low)) + mix(project(high), near(high, 0), far(high))
                + near(low, 2) + chain(low, 0) + chain(high, 2))
    if me == 2:
        return (mix(project(low), far(low), project(high), far(high)) + near(low, 3)
                + near(high[-1:], 1) + chain(low, 1) + chain(high[:-1], 1) + chain(high, 3))
    return (mix(project(low), near(low, 0), far(low)) + mix(project(high), far(high))
            + near(high, 2) + chain(high, 0) + chain(low, 2))


def kernel(
    frames, groups,
    q_hbm, k_hbm, v_hbm, anchor_hbm, w_hbm, mine_ref, direct_ref, chained_ref,
    anchor, q, own, prev, prev2, start, pick, w, att, acc, part, first, onward,
    load_sem, own_sem, w_sem, mine_sem,
    prev_send, prev_recv, prev2_send, prev2_recv, pick_send, start_send, start_recv, go_sem,
    first_send, first_recv, direct_send, direct_recv, chain_send, chain_recv,
):
    f = lax.axis_index("tm")
    h = lax.axis_index("head")
    tokens = q.shape[0]
    heads = q.shape[1] // HS
    chunks, _, width = acc.shape
    rows = tokens // groups
    even = lax.rem(f, 2) == 0
    odd = jnp.logical_not(even)
    has_next, picking = f < frames - 1, even & (f < frames - 3)
    after, after3 = lax.rem(f + 1, frames), lax.rem(f + 3, frames)
    up, down = lax.rem(h + 1, groups), lax.rem(h + groups - 1, groups)

    barrier = pltpu.get_barrier_semaphore()

    @pl.when(f > 0)
    def _():
        pl.semaphore_signal(barrier, inc=1, device_id=(f - 1, h), device_id_type=MESH)

    @pl.when(odd & (f > 1))
    def _():
        pl.semaphore_signal(barrier, inc=1, device_id=(f - 3, h), device_id_type=MESH)

    @pl.when(even & (f > 1))
    def _():
        pl.semaphore_signal(barrier, inc=1, device_id=(f + 1, h), device_id_type=MESH)

    for device in ((f, up), (f, down)):
        pl.semaphore_signal(barrier, inc=1, device_id=device, device_id_type=MESH)

    load_anchor = pltpu.make_async_copy(anchor_hbm, anchor, load_sem.at[0])
    load_q = pltpu.make_async_copy(q_hbm.at[0], q, load_sem.at[1])
    load_w = pltpu.make_async_copy(w_hbm, w, w_sem)
    loads = [[
        pltpu.make_async_copy(ref.at[0, :, pl.ds(c * HS, HS)], own.at[c, i], own_sem.at[c, i])
        for i, ref in enumerate((k_hbm, v_hbm))
    ] for c in range(heads)]
    for c in range(heads):
        for copy in loads[c]:
            copy.start()
    load_anchor.start()
    load_q.start()
    load_w.start()

    @pl.when(f == 0)
    def _():
        prev[...] = jnp.zeros_like(prev)

    @pl.when(f < 2)
    def _():
        start[...] = jnp.zeros_like(start)

    for c in range(heads):
        for copy in loads[c]:
            copy.wait()
    pl.semaphore_wait(
        barrier, 2 + jnp.where(has_next, 1, 0) + jnp.where(picking, 1, 0)
        + jnp.where(odd & (f > 1), 1, 0))

    parts = [(c, i) for c in range(heads) for i in range(2)]
    to_next = [remote(own.at[c], prev.at[c], prev_send.at[c], prev_recv.at[c], (after, h))
               for c in range(heads)]
    passing = [remote(prev.at[c], prev2.at[c], prev2_send.at[c], prev2_recv.at[c], (after, h))
               for c in range(heads)]
    picks = [remote(pick.at[c], start.at[c], pick_send.at[c], start_recv.at[c], (after3, h))
             for c in range(heads)]
    backs = [remote(start.at[c], start.at[c], start_send.at[c], start_recv.at[c],
                    (jnp.maximum(f - 1, 0), h)) for c in range(heads)]

    @pl.when(has_next)
    def _():
        for copy in to_next:
            copy.start()

    load_anchor.wait()
    dist = f - anchor[f]
    load_q.wait()
    scale = HS ** (-0.5)

    starts = jnp.full((tokens, HS), dist, jnp.int32) == 0
    for p in parts:
        if p[1] == 0:
            @pl.when(f > 0)
            def _():
                to_next[p[0]].wait_recv()

        @pl.when(picking)
        def _():
            pick[p] = jnp.where(starts, own[p], prev[p])
            if p[1] == 1:
                picks[p[0]].start()

        if p[1] == 1:
            @pl.when(even & (f > 1))
            def _():
                passing[p[0]].start()

    seen1 = jnp.full((tokens, tokens), dist, jnp.int32) >= 1
    seen2 = jnp.full((tokens, tokens), dist, jnp.int32) >= 2
    state = []
    for c in range(heads):
        query = q[:, c * HS:(c + 1) * HS]
        s0 = dot_nt(query, own[c, 0]) * scale
        s1 = jnp.where(seen1, dot_nt(query, prev[c, 0]) * scale, -jnp.inf)
        top = jnp.max(jnp.maximum(s0, s1), axis=-1, keepdims=True)
        e0, e1 = jnp.exp(s0 - top), jnp.exp(s1 - top)
        total = jnp.sum(e0 + e1, axis=-1, keepdims=True)
        mixed = jnp.dot(e0.astype(BF16), own[c, 1], preferred_element_type=F32)
        mixed += jnp.dot(e1.astype(BF16), prev[c, 1], preferred_element_type=F32)
        state.append((top, total, mixed))

    takes_prev = jnp.full((tokens, HS), jnp.where(odd, dist, 0), jnp.int32) == 2
    half = (heads // 2) * HS

    for c in range(heads):
        if c == heads - 1:
            load_w.wait()
            for j in range(chunks):
                acc[j] = jnp.dot(att[:, :half], w[:half, j * width:(j + 1) * width],
                                 preferred_element_type=F32)

        @pl.when(odd & (f > 1))
        def _():
            picks[c].wait_recv()
            backs[c].start()
            passing[c].wait_recv()

        @pl.when(even & (f > 1))
        def _():
            backs[c].wait_recv()

        query = q[:, c * HS:(c + 1) * HS]
        top, total, mixed = state[c]
        anchor_key = jnp.where(takes_prev, prev2[c, 0], start[c, 0])
        anchor_value = jnp.where(takes_prev, prev2[c, 1], start[c, 1])
        s2 = jnp.where(seen2, dot_nt(query, anchor_key) * scale, -jnp.inf)
        peak = jnp.maximum(top, jnp.max(s2, axis=-1, keepdims=True))
        shrink = jnp.exp(top - peak)
        e2 = jnp.exp(s2 - peak)
        total = total * shrink + jnp.sum(e2, axis=-1, keepdims=True)
        mixed = mixed * shrink + jnp.dot(e2.astype(BF16), anchor_value, preferred_element_type=F32)
        att[:, c * HS:(c + 1) * HS] = (mixed / total).astype(BF16)

    @pl.when(has_next)
    def _():
        for copy in to_next:
            copy.wait_send()

    @pl.when(picking)
    def _():
        for copy in picks:
            copy.wait_send()

    @pl.when((f == 2) | (f == 3))
    def _():
        pl.semaphore_signal(go_sem, inc=1, device_id=(f - 2, h), device_id_type=MESH)

    @pl.when(f < 2)
    def _():
        pl.semaphore_wait(go_sem, 1)

    def columns(j):
        return pl.ds(j * width, width)

    def reduce(me):
        upper, lower, far = (me + 1) % groups, (me - 1) % groups, (me + 2) % groups

        def via(dest, j):
            onward_up = j >= (chunks - 1 if dest == 1 else chunks // 2)
            return (dest - 1 if onward_up else dest + 1) % groups

        def run_of(j, dest):
            length = 4 if dest > 1 else 1
            return range(j // length * length, (j // length + 1) * length)

        def span(run):
            return pl.ds(run[0] * width, len(run) * width)

        def slot(at, dest):
            return 0 if dest == (at - 1) % groups else 1

        def first_copy(run, dest):
            at = via(dest, run[0])
            n = slot(at, dest)
            return remote(part.at[pl.ds(dest * rows, rows), span(run)], first.at[n, :, span(run)],
                          first_send.at[run[0]], first_recv.at[n, run[0]], (f, at))

        def direct_copy(run, dest):
            at = span(run)
            return remote(part.at[pl.ds(dest * rows, rows), at], direct_ref.at[0, :, at],
                          direct_send.at[0 if dest == lower else 1, run[0]],
                          direct_recv.at[run[0]], (f, dest))

        def runs_to(dest):
            source = [(dest - 1) % groups if via(dest, j) != (dest - 1) % groups
                      else (dest + 1) % groups for j in everyone]
            runs = []
            for j in everyone:
                if runs and len(runs[-1]) < 4 and source[runs[-1][0]] == source[j]:
                    runs[-1].append(j)
                else:
                    runs.append([j])
            return runs

        def chain_copy(run, source, dest):
            n = slot(source, dest)
            return remote(onward.at[n, :, span(run)], chained_ref.at[0, :, span(run)],
                          chain_send.at[n, run[0]], chain_recv.at[run[0]], (f, dest))

        def project(j):
            part[:, j * width:(j + 1) * width] = (acc[j] + jnp.dot(att[:, half:], w[half:, j * width:(j + 1) * width],
                                        preferred_element_type=F32)).astype(BF16)

        def chain(run, dest):
            n = slot(me, dest)
            first_copy(run, dest).wait_recv()
            at = slice(run[0] * width, (run[-1] + 1) * width)
            onward[n, :, at] = (part[dest * rows:(dest + 1) * rows, at].astype(F32)
                                + first[n, :, at].astype(F32)).astype(BF16)
            go(chain_copy(run, me, dest))

        def go(copy):
            copy.start()
            sent.append(copy)

        sent, waiting = [], []
        everyone = range(chunks)
        low, high = everyone[:chunks // 2], everyone[chunks // 2:]
        directs = [(j, d) for d in (lower, upper) for j in everyone if via(d, j) != me]
        chains = [(j, d) for d in (lower, upper) for j in everyone if via(d, j) == me]
        plan = plan_of(me, low, high)
        done = set()
        for step in plan:
            kind, j, d = step
            if kind == "P":
                project(j)
            elif kind == "F":
                if j == run_of(j, far)[-1]:
                    go(first_copy(run_of(j, far), far))
            elif kind == "D":
                assert (j, d) in directs
                waiting.append((j, d))
                run = next(r for r in runs_to(d) if j in r)
                if all((k, d) in waiting for k in run):
                    go(direct_copy(run, d))
            else:
                assert (j, d) in chains
                if j == run_of(j, d)[-1]:
                    chain(run_of(j, d), d)
            assert step not in done
            done.add(step)
        assert len(done) == 2 * chunks + len(directs) + len(chains)

        keep = pltpu.make_async_copy
        copy = keep(part.at[pl.ds(me * rows, rows)], mine_ref.at[0], mine_sem)
        copy.start()
        copy.wait()
        for run in runs_to(me):
            at = span(run)
            remote(part.at[pl.ds(me * rows, rows), at], direct_ref.at[0, :, at],
                   direct_send.at[0, run[0]], direct_recv.at[run[0]], (f, lower)).wait_recv()
        for j in everyone:
            if j == run_of(j, me)[0]:
                remote(onward.at[0, :, span(run_of(j, me))], chained_ref.at[0, :, span(run_of(j, me))],
                       chain_send.at[0, j], chain_recv.at[j], (f, lower)).wait_recv()
        for copy in sent:
            copy.wait_send()

    for me in range(groups):
        pl.when(h == me)(functools.partial(reduce, me))

    @pl.when(even & (f > 1))
    def _():
        for copy in passing:
            copy.wait_send()

    @pl.when(odd & (f > 1))
    def _():
        for copy in backs:
            copy.wait_send()


def per_device(frames, groups, queries, keys, values, anchor_of, out_weight):
    _, tokens, wide = queries.shape
    heads = wide // HS
    depth, columns = out_weight.shape
    chunks = 8
    width = columns // chunks
    rows = tokens // groups
    block = pltpu.VMEM((heads, 2, tokens, HS), BF16)
    pieces = pltpu.VMEM((2, rows, columns), BF16)
    dma = pltpu.SemaphoreType.DMA
    hbm = pl.BlockSpec(memory_space=pltpu.HBM)
    anywhere = pl.BlockSpec(memory_space=pl.ANY)
    share = jax.ShapeDtypeStruct((1, rows, columns), BF16)
    mine, direct, chained = pl.pallas_call(
        functools.partial(kernel, frames, groups),
        out_shape=[share] * 3,
        in_specs=[hbm] * 5,
        out_specs=[anywhere] * 3,
        scratch_shapes=[
            pltpu.SMEM(anchor_of.shape, jnp.int32),
            pltpu.VMEM((tokens, wide), BF16),
            block, block, block, block, block,
            pltpu.VMEM((depth, columns), BF16),
            pltpu.VMEM((tokens, wide), BF16),
            pltpu.VMEM((chunks, tokens, width), F32),
            pltpu.VMEM((tokens, columns), BF16),
            pieces, pieces,
            dma((2,)), dma((heads, 2)), dma, dma,
            *[dma((heads,))] * 7, pltpu.SemaphoreType.REGULAR,
            dma((chunks,)), dma((2, chunks)), dma((2, chunks)), dma((chunks,)),
            dma((2, chunks)), dma((chunks,)),
        ],
        compiler_params=pltpu.CompilerParams(
            collective_id=0, has_side_effects=True, vmem_limit_bytes=24 * 2**20),
    )(*(pltpu.with_memory_space_constraint(x, pltpu.HBM)
        for x in (queries, keys, values, anchor_of, out_weight)))
    return (mine.astype(F32) + direct.astype(F32) + chained.astype(F32)).astype(BF16)


def solution(mesh):
    placed = (
        P("tm", None, "head"),
        P("tm", None, "head"),
        P("tm", None, "head"),
        P(),
        P("head", None),
    )
    return jax.shard_map(
        functools.partial(per_device, mesh.shape["tm"], mesh.shape["head"]),
        mesh=mesh, in_specs=placed, out_specs=P("tm", "head", None), check_vma=False
    )
```
